256 devices in a mesh: mem: 32 (over z, x_lo, core), space: 8 (over x_hi, y).
Axes of the slice: x: 4 (x_hi: 2, x_lo: 2; x = x_hi * 2 + x_lo), y: 4, z: 8, core: 2. Of those that a mesh axis runs over, the one named last changes fastest.
Arguments:
- prior_sample_set: float32 [1024, 512, 128], P('mem', 'space'), may hold values from -6 to 6
- perturbed_obs: float32 [1024, 512, 128], P('mem', 'space'), may hold values from -6 to 6
- measured_slot_table: int32 [512, 128], P('space'), may hold values from 0 to 127
- obs_var: float32 [512, 128], P('space'), may hold values from 0.25 to 2
- neighbours: int32 [512, 2], P('space'), may hold values from 0 to 511, as said below
- norm_gain: float32 [64], replicated, may hold values from 0.5 to 1.5
- w_in: bfloat16 [64, 512], replicated, may hold values from -0.75 to 0.75
- b_in: float32 [512], replicated, may hold values from -3 to 3
- w_out: bfloat16 [512, 64], replicated, may hold values from -0.25 to 0.25
- b_out: float32 [64], replicated, may hold values from -1.2 to 1.2
Outputs:
- analysis: float32 [1024, 512, 128], P('mem', 'space')
The draws below stay inside these ranges and needn't reach their ends.
Inputs may be any that keep to these rules, and one draw needn't show every extreme that they name: `neighbours`: row p names 2 different blocks among p - 1, p, p + 1 taken modulo 512, in the order of these offsets. `measured_slot_table`: entry [b, j] names a variable of patch b.
All inputs are finite; a program needn't handle non-finite values.
Results may differ from the reference program's by a relative error of at most 0.0026.
Values sent between devices are 32-bit elements; how exact they have to be, the bound alone decides.
No kernel may reach another device: no remote copies, remote signals or barrier semaphores. Data moves between devices by JAX's collectives and lax.ppermute only.
A program may use at most 64 MiB of HBM per device.

```python
import math
import jax
import jax.numpy as jnp
from jax import lax

LEV = 64
HID = 512
OB = 128
PREDICTION_HOPS = 2
PV = 128
M = 1024
NPATCH = 512


def draw_neighbours(key, part):
    dropped = jax.random.randint(key, (NPATCH,), 0, 3)
    first_offset = jnp.where(dropped == 0, 0, -1)
    second_offset = jnp.where(dropped == 2, 0, 1)
    base = jnp.arange(NPATCH, dtype=jnp.int32)
    offsets = jnp.stack([first_offset, second_offset], axis=1).astype(jnp.int32)
    return ((base[:, None] + offsets) % NPATCH).astype(jnp.int32)


def set_ends(entries, key, least, high):
    extent = entries.shape
    spot = [jax.random.randint(jax.random.fold_in(key, axis), (), 0, extent[axis]) for axis in range(len(extent))]
    entries = entries.at[tuple(spot)].set(least)
    longest = extent.index(max(extent))
    spot[longest] = (spot[longest] + 1) % extent[longest]
    return entries.at[tuple(spot)].set(high)


def block_scale(own_key, extent, pieces, least, high):
    gain = 1.0
    for dim, parts in pieces:
        draws = jax.random.uniform(jax.random.fold_in(jax.random.fold_in(own_key, 6), dim), (parts,), jnp.float32, least / len(pieces), high / len(pieces))
        gain = gain * jnp.repeat(jnp.exp(draws), extent[dim] // parts).reshape((-1,) + (1,) * (len(extent) - 1 - dim))
    return gain


def scatter_about(rng, shape, scale, bound, cuts=(), kind=jnp.bfloat16):
    loudness = block_scale(rng, shape, cuts, -0.22, 0.18) if cuts else 1.0
    values = jax.random.normal(rng, shape, jnp.float32) * scale * loudness
    return jnp.minimum(jnp.maximum(values, -bound), bound).astype(kind)


def setup_inputs(seed: int = 0) -> dict:
    key_of = jax.random.split(jax.random.key(seed), 11)
    prior_sample_set = scatter_about(key_of[0], (M, NPATCH, PV), 1.0, 6.0, ((0, 32), (1, 8)), jnp.float32)
    perturbed_obs = scatter_about(key_of[1], (M, NPATCH, OB), 1.0, 6.0, ((0, 32), (1, 8)), jnp.float32)
    measured_slot_table = set_ends(jax.random.randint(key_of[2], (NPATCH, OB), 0, PV), jax.random.fold_in(key_of[2], 1), 0, PV - 1).astype(jnp.int32)
    obs_var = jnp.clip(jnp.exp(math.log(2.0) - 2.0794415 * jax.random.uniform(key_of[3], (NPATCH, OB), jnp.float32) ** block_scale(key_of[3], (NPATCH, OB), ((0, 8),), -0.2, 0.2)), 0.25, 2.0)
    neighbours = draw_neighbours(jax.random.fold_in(key_of[10], 71), 0)
    norm_gain = jnp.clip(1.0 + 0.1 * jax.random.normal(key_of[5], (LEV,), jnp.float32), 0.5, 1.5)
    w_in = scatter_about(key_of[6], (LEV, HID), LEV ** -0.5, 0.75)
    b_in = scatter_about(key_of[7], (HID,), 0.5, 3.0, (), jnp.float32)
    w_out = scatter_about(key_of[8], (HID, LEV), HID ** -0.5, 0.25)
    b_out = scatter_about(key_of[9], (LEV,), 0.2, 1.2, (), jnp.float32)
    return {"prior_sample_set": prior_sample_set, "perturbed_obs": perturbed_obs, "measured_slot_table": measured_slot_table, "obs_var": obs_var, "neighbours": neighbours, "norm_gain": norm_gain, "w_in": w_in, "b_in": b_in, "w_out": w_out, "b_out": b_out}


def advance(profile_total, norm_gain, w_in, b_in, w_out, b_out):
    for propagate_once in range(PREDICTION_HOPS):
        inverse = lax.rsqrt(lax.optimization_barrier(jnp.mean(profile_total * profile_total, axis=-1, keepdims=True)) + 1e-06)
        normed = (profile_total * inverse * norm_gain).astype(jnp.bfloat16)
        hidden = jax.nn.silu(jnp.dot(normed.astype(jnp.float32), w_in.astype(jnp.float32), preferred_element_type=jnp.float32) + b_in).astype(jnp.bfloat16)
        profile_total = profile_total + jnp.dot(hidden.astype(jnp.float32), w_out.astype(jnp.float32), preferred_element_type=jnp.float32) + b_out
    return profile_total

def update(members, measurement_readings, innovation):
    ensemble_size = members.shape[0]
    anomaly = members - lax.optimization_barrier(jnp.mean(members, axis=0))
    spread = measurement_readings - lax.optimization_barrier(jnp.mean(measurement_readings, axis=0))
    covariance = jnp.dot(spread.T, spread, precision=lax.Precision.HIGHEST) / (ensemble_size - 1)
    covariance = covariance + jnp.eye(measurement_readings.shape[1], dtype=covariance.dtype)
    factor = jnp.linalg.cholesky(covariance)
    partial_solve = lax.linalg.triangular_solve(factor, innovation.T, left_side=True, lower=True)
    weights = lax.linalg.triangular_solve(factor, partial_solve, left_side=True, lower=True, transpose_a=True)
    cross_cov = jnp.dot(anomaly.T, spread, precision=lax.Precision.HIGHEST) / (ensemble_size - 1)
    return members + jnp.dot(cross_cov, weights, precision=lax.Precision.HIGHEST).T

def solve_batch(members, measurement_readings, innovation):
    return jax.vmap(update, in_axes=(1, 1, 1), out_axes=1)(members, measurement_readings, innovation)

def split_pair(picked):
    block_width = picked.shape[-1] // 2
    measurement_readings = picked[..., :block_width].reshape(picked.shape[0], picked.shape[1], -1)
    innovation = picked[..., block_width:].reshape(picked.shape[0], picked.shape[1], -1)
    return (measurement_readings, innovation)

def reference(prior_sample_set, perturbed_obs, measured_slot_table, obs_var, neighbours, norm_gain, w_in, b_in, w_out, b_out):
    profile_total = prior_sample_set.reshape(-1, LEV)
    row_total = profile_total.shape[0]
    block_rows = math.gcd(row_total, 8192)
    stacked = profile_total.reshape(row_total // block_rows, block_rows, LEV)
    propagated_vector = lax.map(lambda piece: advance(piece, norm_gain, w_in, b_in, w_out, b_out), stacked)
    propagate_model_grid = propagated_vector.reshape(prior_sample_set.shape)
    measurement_readings = jnp.take_along_axis(propagate_model_grid, measured_slot_table[None], axis=2)
    weight_root = lax.rsqrt(obs_var)[None]
    paired = jnp.concatenate([measurement_readings * weight_root, (perturbed_obs - measurement_readings) * weight_root], axis=-1)
    batch_sample_total = math.gcd(NPATCH, 8)

    def solve_group(starting_position):
        rows_here = lax.dynamic_slice_in_dim(neighbours, starting_position, batch_sample_total, 0)
        picked = paired[:, rows_here]
        observed_here, innovation_here = split_pair(picked)
        nearby_samples = lax.dynamic_slice_in_dim(propagate_model_grid, starting_position, batch_sample_total, 1)
        return solve_batch(nearby_samples, observed_here, innovation_here)
    firsts = jnp.arange(NPATCH // batch_sample_total, dtype=jnp.int32) * batch_sample_total
    solved = lax.map(solve_group, firsts)
    return jnp.transpose(solved, (1, 0, 2, 3)).reshape(prior_sample_set.shape)
```

```python
import jax
import jax.numpy as jnp
from jax import lax
from jax.experimental import pallas as pl
from jax.experimental.pallas import tpu as pltpu
from jax.sharding import PartitionSpec as P

LEV = 64
HID = 512
HOPS = 2
PV = 128
NMEM = 32
PAIRS = 32
F32 = jnp.float32
BF16 = jnp.bfloat16


def owner_of(pair):
    chip, core = pair // 2, pair % 2
    z, x = (chip, 0) if chip < 8 else (15 - chip, 1)
    return (z * 2 + x) * 2 + core


def pair_of(member):
    z, x, core = member // 4, (member // 2) % 2, member % 2
    return 2 * jnp.where(x == 0, z, 15 - z) + core


def neighbour_moves(step):
    runs = 8
    moves = []
    for run in range(runs):
        for pair in range(PAIRS):
            there = (run * PAIRS + pair + step) % (runs * PAIRS)
            moves.append(
                (owner_of(pair) * runs + run, owner_of(there % PAIRS) * runs + there // PAIRS)
            )
    return moves


def dot(a, b):
    return jnp.dot(a, b, preferred_element_type=F32)


def tdot(a, b):
    return lax.dot_general(a, b, (((0,), (0,)), ((), ())), preferred_element_type=F32)


def split(a):
    high = a.astype(BF16)
    return high, (a - high.astype(F32)).astype(BF16)


def dot3(a, b):
    (ah, al), (bh, bl) = split(a), split(b)
    return dot(ah, bh) + (dot(ah, bl) + dot(al, bh))


def to_send_kernel(x_ref, o_ref):
    for patch in range(2 * PAIRS):
        row = 2 * owner_of(patch // 2) + patch % 2
        o_ref[row] = x_ref[pl.ds(patch, NMEM, stride=2 * PAIRS), :]


def from_sent_kernel(x_ref, o_ref):
    for patch in range(2 * PAIRS):
        row = 2 * owner_of(patch // 2) + patch % 2
        o_ref[pl.ds(patch, NMEM, stride=2 * PAIRS), :] = x_ref[row]


def forecast_kernel(x_ref, g_ref, wi_ref, bi_ref, wo_ref, bo_ref, o_ref, wi2, wo2):
    wi = (wi_ref[...].astype(F32) * 0.5).astype(BF16)
    zi = jnp.zeros_like(wi)
    wi2[:LEV, :HID] = wi
    wi2[:LEV, HID:] = zi
    wi2[LEV:, :HID] = zi
    wi2[LEV:, HID:] = wi
    wo = wo_ref[...]
    zo = jnp.zeros_like(wo)
    wo2[:HID, :] = jnp.concatenate([wo, zo], axis=1)
    wo2[HID:, :] = jnp.concatenate([zo, wo], axis=1)
    gain = jnp.concatenate([g_ref[...]] * 2, axis=1)
    bi = jnp.concatenate([bi_ref[...]] * 2, axis=1) * 0.5
    bo = jnp.concatenate([bo_ref[...]] * 2, axis=1)
    row = lax.broadcasted_iota(jnp.int32, (2 * PV, PV), 0)
    col = lax.broadcasted_iota(jnp.int32, (2 * PV, PV), 1)
    halves = jnp.where((row % PV) // LEV == col // LEV, 1.0, 0.0).astype(BF16)
    chunk = 8
    for first in range(0, 2 * PAIRS, chunk):
        x = jnp.concatenate(
            [x_ref[pl.ds(first + i, NMEM, stride=2 * PAIRS), :] for i in range(chunk)], axis=0
        )
        for _ in range(HOPS):
            squares = jnp.concatenate(split(x * x), axis=1)
            inverse = lax.rsqrt(dot(squares, halves) * (1.0 / LEV) + 1e-6)
            normed = (x * inverse * gain).astype(BF16)
            h = dot(normed, wi2[...]) + bi
            hidden = (h + h * jnp.tanh(h)).astype(BF16)
            x = x + dot(hidden, wo2[...]) + bo
        for i in range(chunk):
            patch = first + i
            o_ref[2 * owner_of(patch // 2) + patch % 2] = x[i * NMEM : (i + 1) * NMEM]


def update_kernel(
    idx_ref, f_ref, fl_ref, fr_ref, p_ref, pl_ref, pr_ref, slot_ref, var_ref, o_ref,
    ah, al, bh, bl, dh, dl, s_ref, x_ref,
):
    members = NMEM * NMEM
    fields = (fl_ref, f_ref.at[:, 0], f_ref.at[:, 1], fr_ref)
    readings = (pl_ref, p_ref.at[:, 0], p_ref.at[:, 1], pr_ref)
    root = lax.rsqrt(var_ref[...])
    for w in range(4):
        x = fields[w][...].reshape(members, PV)
        if w in (1, 2):
            a = x - jnp.mean(x, axis=0, keepdims=True)
            ah[w - 1], al[w - 1] = split(a)
        slots = jnp.broadcast_to(slot_ref[w : w + 1, :], (members, PV))
        y = jnp.take_along_axis(x, slots, axis=1, mode="promise_in_bounds")
        r = root[w : w + 1, :]
        b = (y - jnp.mean(y, axis=0, keepdims=True)) * r
        bh[w], bl[w] = split(b)
        d = (readings[w][...].reshape(members, PV) - y) * r
        dh[w], dl[w] = split(d)
    eye = jnp.where(
        lax.broadcasted_iota(jnp.int32, (2 * PV, 2 * PV), 0)
        == lax.broadcasted_iota(jnp.int32, (2 * PV, 2 * PV), 1),
        1.0,
        0.0,
    )
    scale = 1.0 / (members - 1)
    cross, deltas = [], []
    for j in range(2):
        one, two = idx_ref[j, 0], idx_ref[j, 1]
        rh = jnp.concatenate([bh[one], bh[two]], axis=1)
        rl = jnp.concatenate([bl[one], bl[two]], axis=1)
        mixed = tdot(rh, rl)
        s = (tdot(rh, rh) + (mixed + mixed.T)) * scale + eye
        cross.append((tdot(rh, ah[j]) + (tdot(rh, al[j]) + tdot(rl, ah[j]))) * scale)
        s2 = dot3(s, s)
        top = jnp.max(jnp.sqrt(jnp.sum(jnp.abs(s2), axis=0, keepdims=True)))
        c = 2.0 / (top + 1.0)
        delta = (top - 1.0) / (top + 1.0)
        mu = 2.0 / (2.0 - delta * delta)
        x1 = (mu * c) * (2.0 * eye - c * s)
        t1 = (mu * c) * (2.0 * s - c * s2)
        delta = delta * delta / (2.0 - delta * delta)
        mu = 2.0 / (2.0 - delta * delta)
        s_ref[j] = s
        x_ref[j] = mu * (2.0 * x1 - dot3(x1, t1))
        deltas.append(delta * delta / (2.0 - delta * delta))

    def more(state):
        return jnp.maximum(state[0], state[1]) > 0.02

    def sharpen(state):
        after = []
        for j in range(2):
            delta = state[j]
            x = x_ref[j]
            mu = 2.0 / (2.0 - delta * delta)
            x_ref[j] = mu * (2.0 * x - dot3(x, dot3(s_ref[j], x)))
            after.append(delta * delta / (2.0 - delta * delta))
        return tuple(after)

    lax.while_loop(more, sharpen, tuple(deltas))
    for j in range(2):
        s, x, g = s_ref[j], x_ref[j], cross[j]
        k = dot3(x, g)
        for _ in range(2):
            k = k + dot3(
                x, g - jnp.dot(s, k, precision=lax.Precision.HIGHEST, preferred_element_type=F32)
            )
        kh, kl = split(k)
        one, two = idx_ref[j, 0], idx_ref[j, 1]
        ih = jnp.concatenate([dh[one], dh[two]], axis=1)
        il = jnp.concatenate([dl[one], dl[two]], axis=1)
        gained = dot(ih, kh) + (dot(ih, kl) + dot(il, kh))
        o_ref[:, j] = fields[1 + j][...] + gained.reshape(NMEM, NMEM, PV)


def vmem_call(kernel, out, scratch=(), smem=0, limit=48, n_in=1):
    specs = [pl.BlockSpec(memory_space=pltpu.SMEM)] * smem
    specs += [pl.BlockSpec(memory_space=pltpu.VMEM)] * (n_in - smem)
    return pl.pallas_call(
        kernel,
        out_shape=jax.ShapeDtypeStruct(out, F32),
        in_specs=specs,
        out_specs=pl.BlockSpec(memory_space=pltpu.VMEM),
        scratch_shapes=list(scratch),
        compiler_params=pltpu.CompilerParams(vmem_limit_bytes=limit << 20),
    )


def body(
    prior_sample_set, perturbed_obs, measured_slot_table, obs_var, neighbours,
    norm_gain, w_in, b_in, w_out, b_out,
):
    rows = 2 * PAIRS * NMEM
    sent = (2 * PAIRS, NMEM, PV)
    packed = (NMEM, 2, NMEM, PV)
    both = ("mem", "space")
    first = 2 * pair_of(lax.axis_index("mem"))

    pert_send = vmem_call(to_send_kernel, sent)(perturbed_obs.reshape(rows, PV))
    pert = lax.all_to_all(pert_send.reshape(packed), "mem", 0, 0, tiled=True)

    field_send = vmem_call(
        forecast_kernel, sent,
        [pltpu.VMEM((2 * LEV, 2 * HID), BF16), pltpu.VMEM((2 * HID, 2 * LEV), BF16)], n_in=6,
    )(
        prior_sample_set.reshape(rows, PV), norm_gain.reshape(1, -1), w_in, b_in.reshape(1, -1),
        w_out, b_out.reshape(1, -1),
    )
    meta = jnp.concatenate([measured_slot_table.astype(F32), obs_var], axis=-1)
    field_send, meta = lax.optimization_barrier((field_send, meta))
    field = lax.all_to_all(field_send.reshape(packed), "mem", 0, 0, tiled=True)

    runs = [(i, (i + 1) % 8) for i in range(8)]
    before = lax.ppermute(meta[-1:], "space", runs)
    after = lax.ppermute(meta[:1], "space", [(j, i) for i, j in runs])
    window = lax.dynamic_slice_in_dim(
        jnp.concatenate([before, meta, after], axis=0), first, 4, 0
    )
    slots, variances = window[:, :PV].astype(jnp.int32), window[:, PV:]
    named = lax.dynamic_slice_in_dim(neighbours, first, 2, 0)
    own = jnp.arange(2, dtype=jnp.int32)[:, None]
    place = lax.axis_index("space") * (2 * PAIRS) + first + own
    index = (named - place + 1) % 512 + own

    rightward, leftward = neighbour_moves(1), neighbour_moves(-1)
    pert_left = lax.ppermute(pert[:, 1], both, rightward)
    pert_right = lax.ppermute(pert[:, 0], both, leftward)
    field_left = lax.ppermute(field[:, 1], both, rightward)
    field_right = lax.ppermute(field[:, 0], both, leftward)

    members = NMEM * NMEM
    half = pltpu.VMEM((2, members, PV), BF16)
    full = pltpu.VMEM((4, members, PV), BF16)
    square = pltpu.VMEM((2, 2 * PV, 2 * PV), F32)
    analysis = vmem_call(
        update_kernel, packed, [half, half, full, full, full, full, square, square], smem=1, n_in=9
    )(index, field, field_left, field_right, pert, pert_left, pert_right, slots, variances)
    returned = lax.all_to_all(analysis, "mem", 0, 0, tiled=True)
    out = vmem_call(from_sent_kernel, (rows, PV))(returned.reshape(sent))
    return out.reshape(prior_sample_set.shape)


def solution(mesh):
    rows = P("space", None)
    cube = P("mem", "space", None)
    return jax.shard_map(
        body,
        mesh=mesh,
        in_specs=(cube, cube, rows, rows, rows, P(), P(), P(), P(), P()),
        out_specs=cube,
        check_vma=False,
    )
```

```python
import functools

import jax
import jax.numpy as jnp
from jax import lax
from jax.experimental import pallas as pl
from jax.experimental.pallas import tpu as pltpu
from jax.sharding import PartitionSpec as P

LEV = 64
HID = 512
HOPS = 2
PV = 128
NMEM = 32
PART = 16
PAIRS = 32
F32 = jnp.float32
BF16 = jnp.bfloat16


def owner_of(pair):
    chip, core = pair // 2, pair % 2
    z, x = (chip, 0) if chip < 8 else (15 - chip, 1)
    return (z * 2 + x) * 2 + core


def pair_of(member):
    z, x, core = member // 4, (member // 2) % 2, member % 2
    return 2 * jnp.where(x == 0, z, 15 - z) + core


def neighbour_moves(step):
    runs = 8
    moves = []
    for run in range(runs):
        for pair in range(PAIRS):
            there = (run * PAIRS + pair + step) % (runs * PAIRS)
            moves.append(
                (owner_of(pair) * runs + run, owner_of(there % PAIRS) * runs + there // PAIRS)
            )
    return moves


def dot(a, b):
    return jnp.dot(a, b, preferred_element_type=F32)


def tdot(a, b):
    return lax.dot_general(a, b, (((0,), (0,)), ((), ())), preferred_element_type=F32)


def split(a):
    high = a.astype(BF16)
    return high, (a - high.astype(F32)).astype(BF16)


def dot3(a, b):
    (ah, al), (bh, bl) = split(a), split(b)
    return dot(ah, bh) + (dot(ah, bl) + dot(al, bh))


def to_send_kernel(x_ref, *o_refs):
    for patch in range(2 * PAIRS):
        row = 2 * owner_of(patch // 2) + patch % 2
        for part, o_ref in enumerate(o_refs):
            first = patch + 2 * PAIRS * PART * part
            o_ref[row] = x_ref[pl.ds(first, PART, stride=2 * PAIRS), :]


def from_sent_kernel(x_ref, *rest):
    o_ref = rest[-1]
    for patch in range(2 * PAIRS):
        row = 2 * owner_of(patch // 2) + patch % 2
        o_ref[pl.ds(patch, PART, stride=2 * PAIRS), :] = x_ref[row]


def forecast_kernel(x_ref, g_ref, wi_ref, bi_ref, wo_ref, bo_ref, o_ref, wi2, wo2):
    wi = (wi_ref[...].astype(F32) * 0.5).astype(BF16)
    zi = jnp.zeros_like(wi)
    wi2[:LEV, :HID] = wi
    wi2[:LEV, HID:] = zi
    wi2[LEV:, :HID] = zi
    wi2[LEV:, HID:] = wi
    wo = wo_ref[...]
    zo = jnp.zeros_like(wo)
    wo2[:HID, :] = jnp.concatenate([wo, zo], axis=1)
    wo2[HID:, :] = jnp.concatenate([zo, wo], axis=1)
    gain = jnp.concatenate([g_ref[...]] * 2, axis=1)
    bi = jnp.concatenate([bi_ref[...]] * 2, axis=1) * 0.5
    bo = jnp.concatenate([bo_ref[...]] * 2, axis=1)
    row = lax.broadcasted_iota(jnp.int32, (2 * PV, PV), 0)
    col = lax.broadcasted_iota(jnp.int32, (2 * PV, PV), 1)
    halves = jnp.where((row % PV) // LEV == col // LEV, 1.0, 0.0).astype(BF16)
    chunk = 8
    for first in range(0, 2 * PAIRS, chunk):
        x = jnp.concatenate(
            [x_ref[pl.ds(first + i, NMEM, stride=2 * PAIRS), :] for i in range(chunk)], axis=0
        )
        for _ in range(HOPS):
            squares = jnp.concatenate(split(x * x), axis=1)
            inverse = lax.rsqrt(dot(squares, halves) * (1.0 / LEV) + 1e-6)
            normed = (x * inverse * gain).astype(BF16)
            h = dot(normed, wi2[...]) + bi
            hidden = (h + h * jnp.tanh(h)).astype(BF16)
            x = x + dot(hidden, wo2[...]) + bo
        for i in range(chunk):
            patch = first + i
            o_ref[2 * owner_of(patch // 2) + patch % 2] = x[i * NMEM : (i + 1) * NMEM]


def solve_kernel(
    idx_ref, f_ref, fl_ref, fr_ref, slot_ref, var_ref, k_ref, ah, al, bh, bl, s_ref, x_ref
):
    members = NMEM * NMEM
    fields = (fl_ref, f_ref.at[:, 0], f_ref.at[:, 1], fr_ref)
    root = lax.rsqrt(var_ref[...])
    for w in range(4):
        x = fields[w][...].reshape(members, PV)
        if w in (1, 2):
            a = x - jnp.mean(x, axis=0, keepdims=True)
            ah[w - 1], al[w - 1] = split(a)
        y = observe(x, slot_ref, w)
        b = (y - jnp.mean(y, axis=0, keepdims=True)) * root[w : w + 1, :]
        bh[w], bl[w] = split(b)
    eye = jnp.where(
        lax.broadcasted_iota(jnp.int32, (2 * PV, 2 * PV), 0)
        == lax.broadcasted_iota(jnp.int32, (2 * PV, 2 * PV), 1),
        1.0,
        0.0,
    )
    scale = 1.0 / (members - 1)
    cross, deltas = [], []
    for j in range(2):
        one, two = idx_ref[j, 0], idx_ref[j, 1]
        rh = jnp.concatenate([bh[one], bh[two]], axis=1)
        rl = jnp.concatenate([bl[one], bl[two]], axis=1)
        mixed = tdot(rh, rl)
        s = (tdot(rh, rh) + (mixed + mixed.T)) * scale + eye
        cross.append((tdot(rh, ah[j]) + (tdot(rh, al[j]) + tdot(rl, ah[j]))) * scale)
        s2 = dot3(s, s)
        top = jnp.max(jnp.sqrt(jnp.sum(jnp.abs(s2), axis=0, keepdims=True)))
        c = 2.0 / (top + 1.0)
        delta = (top - 1.0) / (top + 1.0)
        mu = 2.0 / (2.0 - delta * delta)
        x1 = (mu * c) * (2.0 * eye - c * s)
        t1 = (mu * c) * (2.0 * s - c * s2)
        delta = delta * delta / (2.0 - delta * delta)
        mu = 2.0 / (2.0 - delta * delta)
        s_ref[j] = s
        x_ref[j] = mu * (2.0 * x1 - dot3(x1, t1))
        deltas.append(delta * delta / (2.0 - delta * delta))

    def more(state):
        return jnp.maximum(state[0], state[1]) > 0.02

    def sharpen(state):
        after = []
        for j in range(2):
            delta = state[j]
            x = x_ref[j]
            mu = 2.0 / (2.0 - delta * delta)
            x_ref[j] = mu * (2.0 * x - dot3(x, dot3(s_ref[j], x)))
            after.append(delta * delta / (2.0 - delta * delta))
        return tuple(after)

    lax.while_loop(more, sharpen, tuple(deltas))
    for j in range(2):
        s, x, g = s_ref[j], x_ref[j], cross[j]
        k = dot3(x, g)
        for _ in range(2):
            k = k + dot3(
                x, g - jnp.dot(s, k, precision=lax.Precision.HIGHEST, preferred_element_type=F32)
            )
        k_ref[j] = k


def apply_kernel(
    part, idx_ref, k_ref, f_ref, fl_ref, fr_ref, p_ref, pl_ref, pr_ref, slot_ref, var_ref, o_ref,
    dh, dl,
):
    members = NMEM * PART
    here = pl.ds(part * PART, PART)
    fields = (fl_ref.at[:, here], f_ref.at[:, 0, here], f_ref.at[:, 1, here], fr_ref.at[:, here])
    readings = (pl_ref, p_ref.at[:, 0], p_ref.at[:, 1], pr_ref)
    root = lax.rsqrt(var_ref[...])
    for w in range(4):
        y = observe(fields[w][...].reshape(members, PV), slot_ref, w)
        d = (readings[w][...].reshape(members, PV) - y) * root[w : w + 1, :]
        dh[w], dl[w] = split(d)
    for j in range(2):
        kh, kl = split(k_ref[j])
        one, two = idx_ref[j, 0], idx_ref[j, 1]
        ih = jnp.concatenate([dh[one], dh[two]], axis=1)
        il = jnp.concatenate([dl[one], dl[two]], axis=1)
        gained = dot(ih, kh) + (dot(ih, kl) + dot(il, kh))
        o_ref[:, j] = fields[1 + j][...] + gained.reshape(NMEM, PART, PV)


def observe(x, slot_ref, w):
    slots = jnp.broadcast_to(slot_ref[w : w + 1, :], x.shape)
    return jnp.take_along_axis(x, slots, axis=1, mode="promise_in_bounds")


def is_shape(x):
    return isinstance(x, tuple) and isinstance(x[0], int)


def rows_call(part, x, held=None):
    rows = 2 * PAIRS * PART
    specs = [pl.BlockSpec(x.shape, lambda i: (0, 0, 0))]
    if held is not None:
        specs.append(pl.BlockSpec(memory_space=pl.ANY))
    return pl.pallas_call(
        from_sent_kernel,
        grid=(1,),
        out_shape=jax.ShapeDtypeStruct((2 * PAIRS * NMEM, PV), F32),
        in_specs=specs,
        out_specs=pl.BlockSpec((rows, PV), lambda i: (part, 0)),
        input_output_aliases={} if held is None else {1: 0},
        compiler_params=pltpu.CompilerParams(vmem_limit_bytes=16 << 20),
        cost_estimate=pl.CostEstimate(flops=10**9, bytes_accessed=1 << 20, transcendentals=0),
    )(x, *([] if held is None else [held]))


def vmem_call(kernel, out, scratch=(), smem=0, limit=48, n_in=1, us=2):
    specs = [pl.BlockSpec(memory_space=pltpu.SMEM)] * smem
    specs += [pl.BlockSpec(memory_space=pltpu.VMEM)] * (n_in - smem)
    return pl.pallas_call(
        kernel,
        out_shape=jax.tree.map(
            lambda shape: jax.ShapeDtypeStruct(shape, F32), out, is_leaf=is_shape
        ),
        in_specs=specs,
        out_specs=jax.tree.map(
            lambda _: pl.BlockSpec(memory_space=pltpu.VMEM), out, is_leaf=is_shape
        ),
        scratch_shapes=list(scratch),
        compiler_params=pltpu.CompilerParams(vmem_limit_bytes=limit << 20),
        cost_estimate=pl.CostEstimate(
            flops=us * 10**9, bytes_accessed=1 << 20, transcendentals=0
        ),
    )


def body(
    prior_sample_set, perturbed_obs, measured_slot_table, obs_var, neighbours,
    norm_gain, w_in, b_in, w_out, b_out,
):
    rows = 2 * PAIRS * NMEM
    sent = (2 * PAIRS, NMEM, PV)
    packed = (NMEM, 2, NMEM, PV)
    both = ("mem", "space")
    first = 2 * pair_of(lax.axis_index("mem"))

    field_send = vmem_call(
        forecast_kernel, sent,
        [pltpu.VMEM((2 * LEV, 2 * HID), BF16), pltpu.VMEM((2 * HID, 2 * LEV), BF16)], n_in=6, us=8,
    )(
        prior_sample_set.reshape(rows, PV), norm_gain.reshape(1, -1), w_in, b_in.reshape(1, -1),
        w_out, b_out.reshape(1, -1),
    )
    field_send, readings, slot_table, variances, named = lax.optimization_barrier(
        (field_send, perturbed_obs, measured_slot_table, obs_var, neighbours)
    )
    field = lax.all_to_all(field_send.reshape(packed), "mem", 0, 0, tiled=True)

    meta = jnp.concatenate([slot_table.astype(F32), variances], axis=-1)
    runs = [(i, (i + 1) % 8) for i in range(8)]
    before = lax.ppermute(meta[-1:], "space", runs)
    after = lax.ppermute(meta[:1], "space", [(j, i) for i, j in runs])
    window = lax.dynamic_slice_in_dim(
        jnp.concatenate([before, meta, after], axis=0), first, 4, 0
    )
    slots, variances = window[:, :PV].astype(jnp.int32), window[:, PV:]
    own = jnp.arange(2, dtype=jnp.int32)[:, None]
    place = lax.axis_index("space") * (2 * PAIRS) + first + own
    index = (lax.dynamic_slice_in_dim(named, first, 2, 0) - place + 1) % 512 + own
    readings, slots, variances, index = lax.optimization_barrier(
        (readings, slots, variances, index)
    )
    piece = (2 * PAIRS, PART, PV)
    sends = vmem_call(to_send_kernel, (piece, piece))(readings.reshape(rows, PV))

    rightward, leftward = neighbour_moves(1), neighbour_moves(-1)
    field_left = lax.ppermute(field[:, 1], both, rightward)
    field_right = lax.ppermute(field[:, 0], both, leftward)
    packed = (NMEM, 2, PART, PV)
    send, _ = lax.optimization_barrier((sends[0], field))
    pert_a = lax.all_to_all(send.reshape(packed), "mem", 0, 0, tiled=True)
    send, _ = lax.optimization_barrier((sends[1], pert_a))
    pert_b = lax.all_to_all(send.reshape(packed), "mem", 0, 0, tiled=True)

    def halo(pert):
        return lax.ppermute(pert[:, 1], both, rightward), lax.ppermute(pert[:, 0], both, leftward)

    members = NMEM * NMEM
    half = pltpu.VMEM((2, members, PV), BF16)
    full = pltpu.VMEM((4, members, PV), BF16)
    square = pltpu.VMEM((2, 2 * PV, 2 * PV), F32)
    index, _ = lax.optimization_barrier((index, pert_a))
    halo_a = halo(pert_a)
    gain = vmem_call(
        solve_kernel, (2, 2 * PV, PV), [half, half, full, full, square, square], smem=1, n_in=6,
        us=15,
    )(index, field, field_left, field_right, slots, variances)
    pert_b, gain = lax.optimization_barrier((pert_b, gain))
    halo_b = halo(pert_b)

    quarter = pltpu.VMEM((4, NMEM * PART, PV), BF16)
    out = None
    for part, (pert, sides) in enumerate(((pert_a, halo_a), (pert_b, halo_b))):
        analysis = vmem_call(
            functools.partial(apply_kernel, part), packed, [quarter, quarter], smem=1, n_in=10
        )(index, gain, field, field_left, field_right, pert, *sides, slots, variances)
        returned = lax.all_to_all(analysis, "mem", 0, 0, tiled=True)
        out = rows_call(part, returned.reshape(piece), out)
    return out.reshape(prior_sample_set.shape)


def solution(mesh):
    rows = P("space", None)
    cube = P("mem", "space", None)
    return jax.shard_map(
        body,
        mesh=mesh,
        in_specs=(cube, cube, rows, rows, rows, P(), P(), P(), P(), P()),
        out_specs=cube,
        check_vma=False,
    )
```

```python
import jax
import jax.numpy as jnp
from jax import lax
from jax.experimental import pallas as pl
from jax.experimental.pallas import tpu as pltpu
from jax.sharding import PartitionSpec as P

LEV = 64
HID = 512
HOPS = 2
PV = 128
NMEM = 32
STEP = 8
PAIRS = 32
F32 = jnp.float32
BF16 = jnp.bfloat16


def owner_of(pair):
    chip, core = pair // 2, pair % 2
    z, x = (chip, 0) if chip < 8 else (15 - chip, 1)
    return (z * 2 + x) * 2 + core


def pair_of(member):
    z, x, core = member // 4, (member // 2) % 2, member % 2
    return 2 * jnp.where(x == 0, z, 15 - z) + core


def neighbour_moves(step):
    runs = 8
    moves = []
    for run in range(runs):
        for pair in range(PAIRS):
            there = (run * PAIRS + pair + step) % (runs * PAIRS)
            moves.append(
                (owner_of(pair) * runs + run, owner_of(there % PAIRS) * runs + there // PAIRS)
            )
    return moves


def dot(a, b):
    return jnp.dot(a, b, preferred_element_type=F32)


def dot_t(a, b):
    return lax.dot_general(a, b, (((1,), (1,)), ((), ())), preferred_element_type=F32)


def tdot(a, b):
    return lax.dot_general(a, b, (((0,), (0,)), ((), ())), preferred_element_type=F32)


def split(a):
    high = a.astype(BF16)
    return high, (a - high.astype(F32)).astype(BF16)


def dot3(a, b):
    (ah, al), (bh, bl) = split(a), split(b)
    return dot(ah, bh) + (dot(ah, bl) + dot(al, bh))


def to_send_kernel(x_ref, o_ref):
    for patch in range(2 * PAIRS):
        row = 2 * owner_of(patch // 2) + patch % 2
        o_ref[row] = x_ref[pl.ds(patch, NMEM, stride=2 * PAIRS), :]


def from_sent_kernel(x_ref, o_ref):
    for patch in range(2 * PAIRS):
        row = 2 * owner_of(patch // 2) + patch % 2
        o_ref[pl.ds(patch, STEP, stride=2 * PAIRS), :] = x_ref[row]


def forecast_kernel(x_ref, g_ref, wi_ref, bi_ref, wo_ref, bo_ref, o_ref, wi2, wo2):
    for both, one in ((wi2, (wi_ref[...].astype(F32) * 0.5).astype(BF16)), (wo2, wo_ref[...])):
        zero = jnp.zeros_like(one)
        both[:LEV, :HID] = one
        both[:LEV, HID:] = zero
        both[LEV:, :HID] = zero
        both[LEV:, HID:] = one
    gain = jnp.concatenate([g_ref[...]] * 2, axis=1)
    bi = jnp.concatenate([bi_ref[...]] * 2, axis=1) * 0.5
    bo = jnp.concatenate([bo_ref[...]] * 2, axis=1)
    row = lax.broadcasted_iota(jnp.int32, (2 * PV, PV), 0)
    col = lax.broadcasted_iota(jnp.int32, (2 * PV, PV), 1)
    halves = jnp.where((row % PV) // LEV == col // LEV, 1.0, 0.0).astype(BF16)
    chunk = PAIRS
    for first in range(0, 2 * PAIRS, chunk):
        x = jnp.concatenate(
            [x_ref[pl.ds(first + i, NMEM, stride=2 * PAIRS), :] for i in range(chunk)], axis=0
        )
        for _ in range(HOPS):
            squares = jnp.concatenate(split(x * x), axis=1)
            inverse = lax.rsqrt(dot(squares, halves) * (1.0 / LEV) + 1e-6)
            normed = (x * inverse * gain).astype(BF16)
            h = dot(normed, wi2[...]) + bi
            hidden = (h + h * jnp.tanh(h)).astype(BF16)
            x = x + dot_t(hidden, wo2[...]) + bo
        for i in range(chunk):
            patch = first + i
            o_ref[2 * owner_of(patch // 2) + patch % 2] = x[i * NMEM : (i + 1) * NMEM]


def solve_kernel(
    idx_ref, f_ref, fl_ref, fr_ref, slot_ref, var_ref, k_ref, ah, al, bh, bl, s_ref, x_ref
):
    members = NMEM * NMEM
    fields = (fl_ref, f_ref.at[:, 0], f_ref.at[:, 1], fr_ref)
    root = lax.rsqrt(var_ref[...])
    for w in range(4):
        x = fields[w][...].reshape(members, PV)
        if w in (1, 2):
            a = x - jnp.mean(x, axis=0, keepdims=True)
            ah[w - 1], al[w - 1] = split(a)
        y = observe(x, slot_ref, w)
        b = (y - jnp.mean(y, axis=0, keepdims=True)) * root[w : w + 1, :]
        bh[w], bl[w] = split(b)
    eye = jnp.where(
        lax.broadcasted_iota(jnp.int32, (2 * PV, 2 * PV), 0)
        == lax.broadcasted_iota(jnp.int32, (2 * PV, 2 * PV), 1),
        1.0,
        0.0,
    )
    scale = 1.0 / (members - 1)
    cross, deltas = [], []
    for j in range(2):
        one, two = idx_ref[j, 0], idx_ref[j, 1]
        rh = jnp.concatenate([bh[one], bh[two]], axis=1)
        rl = jnp.concatenate([bl[one], bl[two]], axis=1)
        mixed = tdot(rh, rl)
        s = (tdot(rh, rh) + (mixed + mixed.T)) * scale + eye
        cross.append((tdot(rh, ah[j]) + (tdot(rh, al[j]) + tdot(rl, ah[j]))) * scale)
        s2 = dot3(s, s)
        top = jnp.max(jnp.sqrt(jnp.sum(jnp.abs(s2), axis=0, keepdims=True)))
        c = 2.0 / (top + 1.0)
        delta = (top - 1.0) / (top + 1.0)
        mu = 2.0 / (2.0 - delta * delta)
        x1 = (mu * c) * (2.0 * eye - c * s)
        t1 = (mu * c) * (2.0 * s - c * s2)
        delta = delta * delta / (2.0 - delta * delta)
        mu = 2.0 / (2.0 - delta * delta)
        s_ref[j] = s
        x_ref[j] = mu * (2.0 * x1 - dot3(x1, t1))
        deltas.append(delta * delta / (2.0 - delta * delta))

    def more(state):
        return jnp.maximum(state[0], state[1]) > 0.02

    def sharpen(state):
        after = []
        for j in range(2):
            delta = state[j]
            x = x_ref[j]
            mu = 2.0 / (2.0 - delta * delta)
            x_ref[j] = mu * (2.0 * x - dot3(x, dot3(s_ref[j], x)))
            after.append(delta * delta / (2.0 - delta * delta))
        return tuple(after)

    lax.while_loop(more, sharpen, tuple(deltas))
    for j in range(2):
        s, x, g = s_ref[j], x_ref[j], cross[j]
        k = dot3(x, g)
        for _ in range(2):
            k = k + dot3(
                x, g - jnp.dot(s, k, precision=lax.Precision.HIGHEST, preferred_element_type=F32)
            )
        k_ref[j] = k


def apply_kernel(
    idx_ref, k_ref, f_ref, fl_ref, fr_ref, p_ref, pl_ref, pr_ref, slot_ref, var_ref, o_ref, dh, dl
):
    members = NMEM * NMEM
    fields = (fl_ref, f_ref.at[:, 0], f_ref.at[:, 1], fr_ref)
    readings = (pl_ref, p_ref.at[:, 0], p_ref.at[:, 1], pr_ref)
    root = lax.rsqrt(var_ref[...])
    for w in range(4):
        y = observe(fields[w][...].reshape(members, PV), slot_ref, w)
        d = (readings[w][...].reshape(members, PV) - y) * root[w : w + 1, :]
        dh[w], dl[w] = split(d)
    for j in range(2):
        kh, kl = split(k_ref[j])
        one, two = idx_ref[j, 0], idx_ref[j, 1]
        ih = jnp.concatenate([dh[one], dh[two]], axis=1)
        il = jnp.concatenate([dl[one], dl[two]], axis=1)
        gained = dot(ih, kh) + (dot(ih, kl) + dot(il, kh))
        o_ref[:, j] = fields[1 + j][...] + gained.reshape(NMEM, NMEM, PV)


def observe(x, slot_ref, w):
    slots = jnp.broadcast_to(slot_ref[w : w + 1, :], x.shape)
    return jnp.take_along_axis(x, slots, axis=1, mode="promise_in_bounds")


def from_sent(x):
    return pl.pallas_call(
        from_sent_kernel,
        grid=(NMEM // STEP,),
        out_shape=jax.ShapeDtypeStruct((2 * PAIRS * NMEM, PV), F32),
        in_specs=[pl.BlockSpec((2 * PAIRS, STEP, PV), lambda i: (0, i, 0))],
        out_specs=pl.BlockSpec((2 * PAIRS * STEP, PV), lambda i: (i, 0)),
    )(x)


def vmem_call(kernel, out, scratch=(), smem=0, limit=48, n_in=1, us=2):
    specs = [pl.BlockSpec(memory_space=pltpu.SMEM)] * smem
    specs += [pl.BlockSpec(memory_space=pltpu.VMEM)] * (n_in - smem)
    return pl.pallas_call(
        kernel,
        out_shape=jax.ShapeDtypeStruct(out, F32),
        in_specs=specs,
        out_specs=pl.BlockSpec(memory_space=pltpu.VMEM),
        scratch_shapes=list(scratch),
        compiler_params=pltpu.CompilerParams(vmem_limit_bytes=limit << 20),
        cost_estimate=pl.CostEstimate(
            flops=us * 10**9, bytes_accessed=1 << 20, transcendentals=0
        ),
    )


def body(
    prior_sample_set, perturbed_obs, measured_slot_table, obs_var, neighbours,
    norm_gain, w_in, b_in, w_out, b_out,
):
    rows = 2 * PAIRS * NMEM
    sent = (2 * PAIRS, NMEM, PV)
    packed = (NMEM, 2, NMEM, PV)
    both = ("mem", "space")
    first = 2 * pair_of(lax.axis_index("mem"))

    field_send = vmem_call(
        forecast_kernel, sent,
        [pltpu.VMEM((2 * LEV, 2 * HID), BF16)] * 2, n_in=6, us=8,
    )(
        prior_sample_set.reshape(rows, PV), norm_gain.reshape(1, -1), w_in, b_in.reshape(1, -1),
        w_out.T, b_out.reshape(1, -1),
    )
    field_send, readings, slot_table, variances, named = lax.optimization_barrier(
        (field_send, perturbed_obs, measured_slot_table, obs_var, neighbours)
    )
    field = lax.all_to_all(field_send.reshape(packed), "mem", 0, 0, tiled=True)
    meta = jnp.concatenate([slot_table.astype(F32), variances], axis=-1)
    runs = [(i, (i + 1) % 8) for i in range(8)]
    before = lax.ppermute(meta[-1:], "space", runs)
    after = lax.ppermute(meta[:1], "space", [(j, i) for i, j in runs])
    window = lax.dynamic_slice_in_dim(
        jnp.concatenate([before, meta, after], axis=0), first, 4, 0
    )
    slots, variances = window[:, :PV].astype(jnp.int32), window[:, PV:]
    own = jnp.arange(2, dtype=jnp.int32)[:, None]
    place = lax.axis_index("space") * (2 * PAIRS) + first + own
    index = (lax.dynamic_slice_in_dim(named, first, 2, 0) - place + 1) % 512 + own

    readings, slots, variances, index = lax.optimization_barrier(
        (readings, slots, variances, index)
    )
    pert_send = vmem_call(to_send_kernel, sent)(readings.reshape(rows, PV))

    rightward, leftward = neighbour_moves(1), neighbour_moves(-1)
    field_left = lax.ppermute(field[:, 1], both, rightward)
    field_right = lax.ppermute(field[:, 0], both, leftward)
    pert_send, _ = lax.optimization_barrier((pert_send, field))
    pert = lax.all_to_all(pert_send.reshape(packed), "mem", 0, 0, tiled=True)

    members = NMEM * NMEM
    half = pltpu.VMEM((2, members, PV), BF16)
    full = pltpu.VMEM((4, members, PV), BF16)
    square = pltpu.VMEM((2, 2 * PV, 2 * PV), F32)
    gain = vmem_call(
        solve_kernel, (2, 2 * PV, PV), [half, half, full, full, square, square], smem=1, n_in=6,
        us=15,
    )(index, field, field_left, field_right, slots, variances)
    pert, gain = lax.optimization_barrier((pert, gain))
    pert_left = lax.ppermute(pert[:, 1], both, rightward)
    pert_right = lax.ppermute(pert[:, 0], both, leftward)
    analysis = vmem_call(apply_kernel, packed, [full, full], smem=1, n_in=10)(
        index, gain, field, field_left, field_right, pert, pert_left, pert_right, slots, variances
    )
    returned = lax.all_to_all(analysis, "mem", 0, 0, tiled=True)
    out = from_sent(returned.reshape(sent))
    return out.reshape(prior_sample_set.shape)


def solution(mesh):
    rows = P("space", None)
    cube = P("mem", "space", None)
    return jax.shard_map(
        body,
        mesh=mesh,
        in_specs=(cube, cube, rows, rows, rows, P(), P(), P(), P(), P()),
        out_specs=cube,
        check_vma=False,
    )
```

```python
import jax
import jax.numpy as jnp
from jax import lax
from jax.experimental import pallas as pl
from jax.experimental.pallas import tpu as pltpu
from jax.sharding import PartitionSpec as P

LEV = 64
HID = 512
HOPS = 2
PV = 128
NMEM = 32
PAIRS = 32
F32 = jnp.float32
BF16 = jnp.bfloat16


def owner_of(pair):
    chip, core = pair // 2, pair % 2
    z, x = (chip, 0) if chip < 8 else (15 - chip, 1)
    return (z * 2 + x) * 2 + core


def pair_of(member):
    z, x, core = member // 4, (member // 2) % 2, member % 2
    return 2 * jnp.where(x == 0, z, 15 - z) + core


def neighbour_moves(step):
    runs = 8
    moves = []
    for run in range(runs):
        for pair in range(PAIRS):
            there = (run * PAIRS + pair + step) % (runs * PAIRS)
            moves.append(
                (owner_of(pair) * runs + run, owner_of(there % PAIRS) * runs + there // PAIRS)
            )
    return moves


def dot(a, b):
    return jnp.dot(a, b, preferred_element_type=F32)


def dot_t(a, b):
    return lax.dot_general(a, b, (((1,), (1,)), ((), ())), preferred_element_type=F32)


def tdot(a, b):
    return lax.dot_general(a, b, (((0,), (0,)), ((), ())), preferred_element_type=F32)


def split(a):
    high = a.astype(BF16)
    return high, (a - high.astype(F32)).astype(BF16)


def dot3(a, b):
    (ah, al), (bh, bl) = split(a), split(b)
    return dot(ah, bh) + (dot(ah, bl) + dot(al, bh))


def to_send_kernel(x_ref, o_ref):
    for patch in range(2 * PAIRS):
        row = 2 * owner_of(patch // 2) + patch % 2
        o_ref[row] = x_ref[pl.ds(patch, NMEM, stride=2 * PAIRS), :]


def from_sent_kernel(x_ref, o_ref):
    for patch in range(2 * PAIRS):
        row = 2 * owner_of(patch // 2) + patch % 2
        o_ref[pl.ds(patch, NMEM, stride=2 * PAIRS), :] = x_ref[row]


def forecast_kernel(x_ref, g_ref, wi_ref, bi_ref, wo_ref, bo_ref, o_ref, wi2, wo2):
    for both, one in ((wi2, (wi_ref[...].astype(F32) * 0.5).astype(BF16)), (wo2, wo_ref[...])):
        zero = jnp.zeros_like(one)
        both[:LEV, :HID] = one
        both[:LEV, HID:] = zero
        both[LEV:, :HID] = zero
        both[LEV:, HID:] = one
    gain = jnp.concatenate([g_ref[...]] * 2, axis=1)
    bi = jnp.concatenate([bi_ref[...]] * 2, axis=1) * 0.5
    bo = jnp.concatenate([bo_ref[...]] * 2, axis=1)
    row = lax.broadcasted_iota(jnp.int32, (2 * PV, PV), 0)
    col = lax.broadcasted_iota(jnp.int32, (2 * PV, PV), 1)
    halves = jnp.where((row % PV) // LEV == col // LEV, 1.0, 0.0).astype(BF16)
    chunk = PAIRS
    for first in range(0, 2 * PAIRS, chunk):
        x = jnp.concatenate(
            [x_ref[pl.ds(first + i, NMEM, stride=2 * PAIRS), :] for i in range(chunk)], axis=0
        )
        for _ in range(HOPS):
            squares = jnp.concatenate(split(x * x), axis=1)
            inverse = lax.rsqrt(dot(squares, halves) * (1.0 / LEV) + 1e-6)
            normed = (x * inverse * gain).astype(BF16)
            h = dot(normed, wi2[...]) + bi
            hidden = (h + h * jnp.tanh(h)).astype(BF16)
            x = x + dot_t(hidden, wo2[...]) + bo
        for i in range(chunk):
            patch = first + i
            o_ref[2 * owner_of(patch // 2) + patch % 2] = x[i * NMEM : (i + 1) * NMEM]


def exact(a, b):
    return jnp.dot(a, b, precision=lax.Precision.HIGHEST, preferred_element_type=F32)


def observe(x, slots):
    slots = jnp.broadcast_to(slots, x.shape)
    return jnp.take_along_axis(x, slots, axis=1, mode="promise_in_bounds")


def centred(x):
    return x - jnp.mean(x, axis=0, keepdims=True)


def identity():
    row = lax.broadcasted_iota(jnp.int32, (PV, PV), 0)
    return jnp.where(row == lax.broadcasted_iota(jnp.int32, (PV, PV), 1), 1.0, 0.0)


def inverses(matrices, s_ref, x_ref):
    deltas = []
    eye = identity()
    for j, s in enumerate(matrices):
        s2 = dot3(s, s)
        top = jnp.max(jnp.sqrt(jnp.sum(jnp.abs(s2), axis=0, keepdims=True)))
        c = 2.0 / (top + 1.0)
        delta = (top - 1.0) / (top + 1.0)
        mu = 2.0 / (2.0 - delta * delta)
        x1 = (mu * c) * (2.0 * eye - c * s)
        t1 = (mu * c) * (2.0 * s - c * s2)
        delta = delta * delta / (2.0 - delta * delta)
        mu = 2.0 / (2.0 - delta * delta)
        s_ref[j] = s
        x_ref[j] = mu * (2.0 * x1 - dot3(x1, t1))
        deltas.append(delta * delta / (2.0 - delta * delta))

    def more(state):
        return jnp.maximum(state[0], state[1]) > 0.02

    def sharpen(state):
        after = []
        for j in range(2):
            delta = state[j]
            x = x_ref[j]
            mu = 2.0 / (2.0 - delta * delta)
            x_ref[j] = mu * (2.0 * x - dot3(x, dot3(s_ref[j], x)))
            after.append(delta * delta / (2.0 - delta * delta))
        return tuple(after)

    lax.while_loop(more, sharpen, tuple(deltas))


def own_kernel(
    idx_ref, f_ref, p_ref, slot_ref, var_ref,
    ah, al, bh, bl, dh, dl, inv_ref, part_ref, s_ref, x_ref,
):
    members = NMEM * NMEM
    root = lax.rsqrt(var_ref[...])
    for w in range(2):
        x = f_ref[:, w].reshape(members, PV)
        y = observe(x, slot_ref[w + 1 : w + 2, :])
        r = root[w + 1 : w + 2, :]
        ah[w], al[w] = split(centred(x))
        bh[w], bl[w] = split(centred(y) * r)
        dh[w], dl[w] = split((p_ref[:, w].reshape(members, PV) - y) * r)
    scale = 1.0 / (members - 1)
    matrices, crosses = [], []
    for j in range(2):
        o = idx_ref[j, 0] - 1
        high, low = bh[o], bl[o]
        mixed = tdot(high, low)
        matrices.append((tdot(high, high) + (mixed + mixed.T)) * scale + identity())
        crosses.append((tdot(high, ah[j]) + (tdot(high, al[j]) + tdot(low, ah[j]))) * scale)
    inverses(matrices, s_ref, x_ref)
    for j in range(2):
        s, x = s_ref[j], x_ref[j]
        x = 2.0 * x - dot3(x, dot3(s, x))
        x = 2.0 * x - exact(x, exact(s, x))
        inv_ref[j] = x
        part_ref[j] = exact(x, crosses[j])


def update_kernel(
    idx_ref, f_ref, fl_ref, fr_ref, p_ref, pl_ref, pr_ref, slot_ref, var_ref,
    ah, al, bh, bl, dh, dl, inv_ref, part_ref, o_ref, hh, hl, s_ref, x_ref,
):
    members = NMEM * NMEM
    scale = 1.0 / (members - 1)
    fields, readings = (fl_ref, fr_ref), (pl_ref, pr_ref)
    complements, links, crosses = [], [], []
    for j in range(2):
        o, h = idx_ref[j, 0] - 1, idx_ref[j, 1]
        apart = h == 3 * j
        x = jnp.where(apart, fields[j][...], f_ref[:, j]).reshape(members, PV)
        p = jnp.where(apart, readings[j][...], p_ref[:, j]).reshape(members, PV)
        y = observe(x, slot_ref[pl.ds(h, 1), :])
        r = lax.rsqrt(var_ref[pl.ds(h, 1), :])
        high, low = split(centred(y) * r)
        hh[j], hl[j] = split((p - y) * r)
        right = jnp.concatenate([bh[o], high, ah[j]], axis=1)
        under = jnp.concatenate([bl[o], low, al[j]], axis=1)
        gram = (tdot(high, right) + (tdot(high, under) + tdot(low, right))) * scale
        s_ho, s_hh, g_h = gram[:, :PV], gram[:, PV : 2 * PV] + identity(), gram[:, 2 * PV :]
        link = dot3(s_ho, inv_ref[j])
        complements.append(s_hh - dot3(link, s_ho.T))
        links.append(link)
        crosses.append(g_h - dot3(s_ho, part_ref[j]))
    inverses(complements, s_ref, x_ref)
    for j in range(2):
        s, x, g = s_ref[j], x_ref[j], crosses[j]
        k_h = dot3(x, g)
        for _ in range(2):
            k_h = k_h + dot3(x, g - exact(s, k_h))
        k_o = part_ref[j] - dot3(links[j].T, k_h)
        kh, kl = split(jnp.concatenate([k_o, k_h], axis=0))
        o = idx_ref[j, 0] - 1
        ih = jnp.concatenate([dh[o], hh[j]], axis=1)
        il = jnp.concatenate([dl[o], hl[j]], axis=1)
        gained = dot(ih, kh) + (dot(ih, kl) + dot(il, kh))
        o_ref[:, j] = f_ref[:, j] + gained.reshape(NMEM, NMEM, PV)


def vmem_call(kernel, out, scratch=(), smem=0, limit=24, n_in=1, us=2):
    specs = [pl.BlockSpec(memory_space=pltpu.SMEM)] * smem
    specs += [pl.BlockSpec(memory_space=pltpu.VMEM)] * (n_in - smem)
    single = isinstance(out, tuple)
    shapes = jax.ShapeDtypeStruct(out, F32) if single else out
    return pl.pallas_call(
        kernel,
        out_shape=shapes,
        in_specs=specs,
        out_specs=jax.tree.map(lambda _: pl.BlockSpec(memory_space=pltpu.VMEM), shapes),
        scratch_shapes=list(scratch),
        compiler_params=pltpu.CompilerParams(vmem_limit_bytes=limit << 20),
        cost_estimate=pl.CostEstimate(
            flops=us * 10**9, bytes_accessed=1 << 20, transcendentals=0
        ),
    )


def body(
    prior_sample_set, perturbed_obs, measured_slot_table, obs_var, neighbours,
    norm_gain, w_in, b_in, w_out, b_out,
):
    rows = 2 * PAIRS * NMEM
    sent = (2 * PAIRS, NMEM, PV)
    packed = (NMEM, 2, NMEM, PV)
    both = ("mem", "space")
    first = 2 * pair_of(lax.axis_index("mem"))

    pert_send = vmem_call(to_send_kernel, sent)(perturbed_obs.reshape(rows, PV))
    pert = lax.all_to_all(pert_send.reshape(packed), "mem", 0, 0, tiled=True)

    field_send = vmem_call(
        forecast_kernel, sent,
        [pltpu.VMEM((2 * LEV, 2 * HID), BF16)] * 2, n_in=6, us=7,
    )(
        prior_sample_set.reshape(rows, PV), norm_gain.reshape(1, -1), w_in, b_in.reshape(1, -1),
        w_out.T, b_out.reshape(1, -1),
    )
    meta = jnp.concatenate([measured_slot_table.astype(F32), obs_var], axis=-1)
    field_send, meta = lax.optimization_barrier((field_send, meta))
    field = lax.all_to_all(field_send.reshape(packed), "mem", 0, 0, tiled=True)

    runs = [(i, (i + 1) % 8) for i in range(8)]
    before = lax.ppermute(meta[-1:], "space", runs)
    after = lax.ppermute(meta[:1], "space", [(j, i) for i, j in runs])
    window = lax.dynamic_slice_in_dim(
        jnp.concatenate([before, meta, after], axis=0), first, 4, 0
    )
    slots, variances = window[:, :PV].astype(jnp.int32), window[:, PV:]
    named = lax.dynamic_slice_in_dim(neighbours, first, 2, 0)
    own = jnp.arange(2, dtype=jnp.int32)[:, None]
    place = lax.axis_index("space") * (2 * PAIRS) + first + own
    index = (named - place + 1) % 512 + own

    rightward, leftward = neighbour_moves(1), neighbour_moves(-1)
    pert_left = lax.ppermute(pert[:, 1], both, rightward)
    pert_right = lax.ppermute(pert[:, 0], both, leftward)
    field_left = lax.ppermute(field[:, 1], both, rightward)
    field_right = lax.ppermute(field[:, 0], both, leftward)

    members = NMEM * NMEM
    pair = jax.ShapeDtypeStruct((2, members, PV), BF16)
    small = jax.ShapeDtypeStruct((2, PV, PV), F32)
    half = pltpu.VMEM((2, members, PV), BF16)
    square = pltpu.VMEM((2, PV, PV), F32)
    index = jnp.concatenate([index[:1, ::-1], index[1:]], axis=0)
    own_parts = vmem_call(
        own_kernel, [pair] * 6 + [small] * 2, [square, square], smem=1, n_in=5, us=9
    )(index, field, pert, slots, variances)
    analysis = vmem_call(update_kernel, packed, [half, half, square, square], smem=1, n_in=17, us=7)(
        index, field, field_left, field_right, pert, pert_left, pert_right, slots, variances,
        *own_parts,
    )
    returned = lax.all_to_all(analysis, "mem", 0, 0, tiled=True)
    out = vmem_call(from_sent_kernel, (rows, PV))(returned.reshape(sent))
    return out.reshape(prior_sample_set.shape)


def solution(mesh):
    rows = P("space", None)
    cube = P("mem", "space", None)
    return jax.shard_map(
        body,
        mesh=mesh,
        in_specs=(cube, cube, rows, rows, rows, P(), P(), P(), P(), P()),
        out_specs=cube,
        check_vma=False,
    )
```

```python
import jax
import jax.numpy as jnp
from jax import lax
from jax.experimental import pallas as pl
from jax.experimental.pallas import tpu as pltpu
from jax.sharding import PartitionSpec as P

LEV = 64
HID = 512
HOPS = 2
PV = 128
NMEM = 32
PIECES = 4
PAIRS = 32
F32 = jnp.float32
BF16 = jnp.bfloat16


def owner_of(pair):
    chip, core = pair // 2, pair % 2
    z, x = (chip, 0) if chip < 8 else (15 - chip, 1)
    return (z * 2 + x) * 2 + core


def pair_of(member):
    z, x, core = member // 4, (member // 2) % 2, member % 2
    return 2 * jnp.where(x == 0, z, 15 - z) + core


def neighbour_moves(step):
    runs = 8
    moves = []
    for run in range(runs):
        for pair in range(PAIRS):
            there = (run * PAIRS + pair + step) % (runs * PAIRS)
            moves.append(
                (owner_of(pair) * runs + run, owner_of(there % PAIRS) * runs + there // PAIRS)
            )
    return moves


def dot(a, b):
    return jnp.dot(a, b, preferred_element_type=F32)


def dot_t(a, b):
    return lax.dot_general(a, b, (((1,), (1,)), ((), ())), preferred_element_type=F32)


def tdot(a, b):
    return lax.dot_general(a, b, (((0,), (0,)), ((), ())), preferred_element_type=F32)


def split(a):
    high = a.astype(BF16)
    return high, (a - high.astype(F32)).astype(BF16)


def dot3(a, b):
    (ah, al), (bh, bl) = split(a), split(b)
    return dot(ah, bh) + (dot(ah, bl) + dot(al, bh))


def sent_row(patch):
    return 2 * owner_of(patch // 2) + patch % 2


def to_send_kernel(x_ref, o_ref, came, put, in_sems, out_sems):
    group = 2 * PAIRS // PIECES
    for g in range(PIECES):
        part = pl.ds(g * group, group)
        pltpu.make_async_copy(x_ref.at[:, part], came.at[:, part], in_sems.at[g]).start()
    rows = came.reshape(2 * PAIRS * NMEM, PV)
    copies = []
    for g in range(PIECES):
        part = pl.ds(g * group, group)
        pltpu.make_async_copy(x_ref.at[:, part], came.at[:, part], in_sems.at[g]).wait()
        for chip in range(g * group // 4, (g + 1) * group // 4):
            for patch in range(4 * chip, 4 * chip + 4):
                put[sent_row(patch)] = rows[pl.ds(patch, NMEM, stride=2 * PAIRS), :]
            part = pl.ds(sent_row(4 * chip), 4)
            copies.append(pltpu.make_async_copy(put.at[part], o_ref.at[part], out_sems.at[chip]))
            copies[-1].start()
    for copy in copies:
        copy.wait()


def from_sent_kernel(x_ref, o_ref, put, sems):
    step = NMEM // PIECES
    copies = []
    for g in range(PIECES):
        first = g * step * 2 * PAIRS
        for patch in range(2 * PAIRS):
            put[pl.ds(first + patch, step, stride=2 * PAIRS), :] = x_ref[
                sent_row(patch), g * step : (g + 1) * step
            ]
        part = pl.ds(first, step * 2 * PAIRS)
        copies.append(pltpu.make_async_copy(put.at[part], o_ref.at[part], sems.at[g]))
        copies[-1].start()
    for copy in copies:
        copy.wait()


def forecast_kernel(x_ref, g_ref, wi_ref, bi_ref, wo_ref, bo_ref, o_ref, wi2, wo2):
    for both, one in ((wi2, (wi_ref[...].astype(F32) * 0.5).astype(BF16)), (wo2, wo_ref[...])):
        zero = jnp.zeros_like(one)
        both[:LEV, :HID] = one
        both[:LEV, HID:] = zero
        both[LEV:, :HID] = zero
        both[LEV:, HID:] = one
    gain = jnp.concatenate([g_ref[...]] * 2, axis=1)
    bi = jnp.concatenate([bi_ref[...]] * 2, axis=1) * 0.5
    bo = jnp.concatenate([bo_ref[...]] * 2, axis=1)
    row = lax.broadcasted_iota(jnp.int32, (2 * PV, PV), 0)
    col = lax.broadcasted_iota(jnp.int32, (2 * PV, PV), 1)
    halves = jnp.where((row % PV) // LEV == col // LEV, 1.0, 0.0).astype(BF16)
    chunk = PAIRS
    for first in range(0, 2 * PAIRS, chunk):
        x = jnp.concatenate(
            [x_ref[pl.ds(first + i, NMEM, stride=2 * PAIRS), :] for i in range(chunk)], axis=0
        )
        for _ in range(HOPS):
            squares = jnp.concatenate(split(x * x), axis=1)
            inverse = lax.rsqrt(dot(squares, halves) * (1.0 / LEV) + 1e-6)
            normed = (x * inverse * gain).astype(BF16)
            h = dot(normed, wi2[...]) + bi
            hidden = (h + h * jnp.tanh(h)).astype(BF16)
            x = x + dot_t(hidden, wo2[...]) + bo
        for i in range(chunk):
            patch = first + i
            o_ref[sent_row(patch)] = x[i * NMEM : (i + 1) * NMEM]


def exact(a, b):
    return jnp.dot(a, b, precision=lax.Precision.HIGHEST, preferred_element_type=F32)


def observe(x, slots):
    slots = jnp.broadcast_to(slots, x.shape)
    return jnp.take_along_axis(x, slots, axis=1, mode="promise_in_bounds")


def centred(x):
    return x - jnp.mean(x, axis=0, keepdims=True)


def identity():
    row = lax.broadcasted_iota(jnp.int32, (PV, PV), 0)
    return jnp.where(row == lax.broadcasted_iota(jnp.int32, (PV, PV), 1), 1.0, 0.0)


def inverses(matrices, s_ref, x_ref):
    deltas = []
    eye = identity()
    for j, s in enumerate(matrices):
        s2 = dot3(s, s)
        norms = jnp.sum(jnp.abs(s2), axis=0, keepdims=True)
        top = jnp.sqrt(jnp.max(norms, axis=1, keepdims=True))
        c = 2.0 / (top + 1.0)
        delta = (top - 1.0) / (top + 1.0)
        mu = 2.0 / (2.0 - delta * delta)
        x1 = (mu * c) * (2.0 * eye - c * s)
        t1 = (mu * c) * (2.0 * s - c * s2)
        delta = delta * delta / (2.0 - delta * delta)
        mu = 2.0 / (2.0 - delta * delta)
        s_ref[j] = s
        x_ref[j] = mu * (2.0 * x1 - dot3(x1, t1))
        deltas.append(jnp.max(delta * delta / (2.0 - delta * delta)))

    def more(state):
        return jnp.maximum(state[0], state[1]) > 0.02

    def sharpen(state):
        after = []
        for j in range(2):
            delta = state[j]
            x = x_ref[j]
            mu = 2.0 / (2.0 - delta * delta)
            x_ref[j] = mu * (2.0 * x - dot3(x, dot3(s_ref[j], x)))
            after.append(delta * delta / (2.0 - delta * delta))
        return tuple(after)

    lax.while_loop(more, sharpen, tuple(deltas))


def own_kernel(
    idx_ref, f_ref, p_ref, slot_ref, var_ref,
    ah, al, bh, bl, dh, dl, inv_ref, part_ref, base_ref, s_ref, x_ref,
):
    members = NMEM * NMEM
    root = lax.rsqrt(var_ref[...])
    for w in range(2):
        x = f_ref[:, w].reshape(members, PV)
        y = observe(x, slot_ref[w + 1 : w + 2, :])
        r = root[w + 1 : w + 2, :]
        ah[w], al[w] = split(centred(x))
        bh[w], bl[w] = split(centred(y) * r)
        dh[w], dl[w] = split((p_ref[:, w].reshape(members, PV) - y) * r)
    scale = 1.0 / (members - 1)
    matrices, crosses = [], []
    for j in range(2):
        o = idx_ref[j, 0] - 1
        high, low = bh[o], bl[o]
        mixed = tdot(high, low)
        matrices.append((tdot(high, high) + (mixed + mixed.T)) * scale + identity())
        crosses.append((tdot(high, ah[j]) + (tdot(high, al[j]) + tdot(low, ah[j]))) * scale)
    inverses(matrices, s_ref, x_ref)
    for j in range(2):
        s, x = s_ref[j], x_ref[j]
        x = 2.0 * x - dot3(x, dot3(s, x))
        x = 2.0 * x - exact(x, exact(s, x))
        inv_ref[j] = x
        part = exact(x, crosses[j])
        part_ref[j] = part
        o = idx_ref[j, 0] - 1
        ph, pl_ = split(part)
        gained = dot(dh[o], ph) + (dot(dh[o], pl_) + dot(dl[o], ph))
        base_ref[:, j] = f_ref[:, j] + gained.reshape(NMEM, NMEM, PV)


def update_kernel(
    idx_ref, f_ref, fl_ref, fr_ref, p_ref, pl_ref, pr_ref, slot_ref, var_ref,
    ah, al, bh, bl, dh, dl, inv_ref, part_ref, base_ref, o_ref, hh, hl, s_ref, x_ref,
):
    members = NMEM * NMEM
    scale = 1.0 / (members - 1)
    fields, readings = (fl_ref, fr_ref), (pl_ref, pr_ref)
    complements, crosses = [], []
    for j in range(2):
        o, h = idx_ref[j, 0] - 1, idx_ref[j, 1]
        apart = h == 3 * j
        x = jnp.where(apart, fields[j][...], f_ref[:, j]).reshape(members, PV)
        p = jnp.where(apart, readings[j][...], p_ref[:, j]).reshape(members, PV)
        y = observe(x, slot_ref[pl.ds(h, 1), :])
        r = lax.rsqrt(var_ref[pl.ds(h, 1), :])
        high, low = split(centred(y) * r)
        right = jnp.concatenate([bh[o], high, ah[j]], axis=1)
        under = jnp.concatenate([bl[o], low, al[j]], axis=1)
        gram = (tdot(high, right) + (tdot(high, under) + tdot(low, right))) * scale
        s_ho, s_hh, g_h = gram[:, :PV], gram[:, PV : 2 * PV] + identity(), gram[:, 2 * PV :]
        link = dot3(s_ho, inv_ref[j])
        complements.append(s_hh - dot3(link, s_ho.T))
        crosses.append(g_h - dot3(s_ho, part_ref[j]))
        lh, ll = split(link)
        carried = dot_t(dh[o], lh) + (dot_t(dh[o], ll) + dot_t(dl[o], lh))
        hh[j], hl[j] = split((p - y) * r - carried)
    inverses(complements, s_ref, x_ref)
    for j in range(2):
        s, x, g = s_ref[j], x_ref[j], crosses[j]
        k_h = dot3(x, g)
        for _ in range(2):
            k_h = k_h + dot3(x, g - exact(s, k_h))
        kh, kl = split(k_h)
        gained = dot(hh[j], kh) + (dot(hh[j], kl) + dot(hl[j], kh))
        o_ref[:, j] = base_ref[:, j] + gained.reshape(NMEM, NMEM, PV)


def copying_call(kernel, out, space, scratch, limit=16):
    return pl.pallas_call(
        kernel,
        out_shape=jax.ShapeDtypeStruct(out, F32),
        in_specs=[pl.BlockSpec(memory_space=space)],
        out_specs=pl.BlockSpec(memory_space=pl.ANY),
        scratch_shapes=scratch,
        compiler_params=pltpu.CompilerParams(vmem_limit_bytes=limit << 20),
        cost_estimate=pl.CostEstimate(flops=10**9, bytes_accessed=2 << 20, transcendentals=0),
    )


def vmem_call(kernel, out, scratch=(), smem=0, limit=24, n_in=1, us=2):
    specs = [pl.BlockSpec(memory_space=pltpu.SMEM)] * smem
    specs += [pl.BlockSpec(memory_space=pltpu.VMEM)] * (n_in - smem)
    single = isinstance(out, tuple)
    shapes = jax.ShapeDtypeStruct(out, F32) if single else out
    return pl.pallas_call(
        kernel,
        out_shape=shapes,
        in_specs=specs,
        out_specs=jax.tree.map(lambda _: pl.BlockSpec(memory_space=pltpu.VMEM), shapes),
        scratch_shapes=list(scratch),
        compiler_params=pltpu.CompilerParams(vmem_limit_bytes=limit << 20),
        cost_estimate=pl.CostEstimate(
            flops=us * 10**9, bytes_accessed=1 << 20, transcendentals=0
        ),
    )


def body(
    prior_sample_set, perturbed_obs, measured_slot_table, obs_var, neighbours,
    norm_gain, w_in, b_in, w_out, b_out,
):
    rows = 2 * PAIRS * NMEM
    sent = (2 * PAIRS, NMEM, PV)
    packed = (NMEM, 2, NMEM, PV)
    both = ("mem", "space")
    first = 2 * pair_of(lax.axis_index("mem"))

    pert_send = copying_call(
        to_send_kernel, sent, pl.ANY,
        [
            pltpu.VMEM(perturbed_obs.shape, F32), pltpu.VMEM(sent, F32),
            pltpu.SemaphoreType.DMA((PIECES,)), pltpu.SemaphoreType.DMA((PAIRS // 2,)),
        ],
        limit=60,
    )(perturbed_obs)
    pert = lax.all_to_all(pert_send.reshape(packed), "mem", 0, 0, tiled=True)

    field_send = vmem_call(
        forecast_kernel, sent,
        [pltpu.VMEM((2 * LEV, 2 * HID), BF16)] * 2, n_in=6, us=7,
    )(
        prior_sample_set.reshape(rows, PV), norm_gain.reshape(1, -1), w_in, b_in.reshape(1, -1),
        w_out.T, b_out.reshape(1, -1),
    )
    meta = jnp.concatenate([measured_slot_table.astype(F32), obs_var], axis=-1)
    field_send, meta = lax.optimization_barrier((field_send, meta))
    field = lax.all_to_all(field_send.reshape(packed), "mem", 0, 0, tiled=True)

    runs = [(i, (i + 1) % 8) for i in range(8)]
    before = lax.ppermute(meta[-1:], "space", runs)
    after = lax.ppermute(meta[:1], "space", [(j, i) for i, j in runs])
    window = lax.dynamic_slice_in_dim(
        jnp.concatenate([before, meta, after], axis=0), first, 4, 0
    )
    slots, variances = window[:, :PV].astype(jnp.int32), window[:, PV:]
    named = lax.dynamic_slice_in_dim(neighbours, first, 2, 0)
    own = jnp.arange(2, dtype=jnp.int32)[:, None]
    place = lax.axis_index("space") * (2 * PAIRS) + first + own
    index = (named - place + 1) % 512 + own

    rightward, leftward = neighbour_moves(1), neighbour_moves(-1)
    pert_left = lax.ppermute(pert[:, 1], both, rightward)
    pert_right = lax.ppermute(pert[:, 0], both, leftward)
    field_left = lax.ppermute(field[:, 1], both, rightward)
    field_right = lax.ppermute(field[:, 0], both, leftward)

    members = NMEM * NMEM
    pair = jax.ShapeDtypeStruct((2, members, PV), BF16)
    small = jax.ShapeDtypeStruct((2, PV, PV), F32)
    base = jax.ShapeDtypeStruct(packed, F32)
    half = pltpu.VMEM((2, members, PV), BF16)
    square = pltpu.VMEM((2, PV, PV), F32)
    index = jnp.concatenate([index[:1, ::-1], index[1:]], axis=0)
    own_parts = vmem_call(
        own_kernel, [pair] * 6 + [small] * 2 + [base], [square, square], smem=1, n_in=5, us=9
    )(index, field, pert, slots, variances)
    analysis = vmem_call(update_kernel, packed, [half, half, square, square], smem=1, n_in=18, us=7)(
        index, field, field_left, field_right, pert, pert_left, pert_right, slots, variances,
        *own_parts,
    )
    returned = lax.all_to_all(analysis, "mem", 0, 0, tiled=True)
    out = copying_call(
        from_sent_kernel, (rows, PV), pltpu.VMEM,
        [pltpu.VMEM((rows, PV), F32), pltpu.SemaphoreType.DMA((PIECES,))],
    )(returned.reshape(sent))
    return out.reshape(prior_sample_set.shape)


def solution(mesh):
    rows = P("space", None)
    cube = P("mem", "space", None)
    return jax.shard_map(
        body,
        mesh=mesh,
        in_specs=(cube, cube, rows, rows, rows, P(), P(), P(), P(), P()),
        out_specs=cube,
        check_vma=False,
    )
```

```python
import jax
import jax.numpy as jnp
from jax import lax
from jax.experimental import pallas as pl
from jax.experimental.pallas import tpu as pltpu
from jax.sharding import PartitionSpec as P

LEV = 64
HID = 512
HOPS = 2
PV = 128
NMEM = 32
PIECES = 4
PAIRS = 32
F32 = jnp.float32
BF16 = jnp.bfloat16


def owner_of(pair):
    chip, core = pair // 2, pair % 2
    z, x = (chip, 0) if chip < 8 else (15 - chip, 1)
    return (z * 2 + x) * 2 + core


def mirrored(run):
    return (run + 1 + run // 4) % 2


def pair_of(member, run):
    z, x, core = member // 4, (member // 2 + mirrored(run)) % 2, member % 2
    return 2 * jnp.where(x == 0, z, 15 - z) + core


def neighbour_moves(step):
    runs = 8

    def device(patches):
        run, pair = patches // PAIRS % runs, patches % PAIRS
        return (owner_of(pair) ^ 2 * mirrored(run)) * runs + run

    return [(device(here), device(here + step)) for here in range(runs * PAIRS)]


def dot(a, b):
    return jnp.dot(a, b, preferred_element_type=F32)


def dot_t(a, b):
    return lax.dot_general(a, b, (((1,), (1,)), ((), ())), preferred_element_type=F32)


def tdot(a, b):
    return lax.dot_general(a, b, (((0,), (0,)), ((), ())), preferred_element_type=F32)


def split(a):
    high = a.astype(BF16)
    return high, (a - high.astype(F32)).astype(BF16)


def dot3(a, b):
    (ah, al), (bh, bl) = split(a), split(b)
    return dot(ah, bh) + (dot(ah, bl) + dot(al, bh))


def row_shift():
    return 4 * mirrored(lax.axis_index("space"))


def sent_row(patch, shift):
    row = 2 * owner_of(patch // 2) + patch % 2
    return row - shift if row & 4 else row + shift


def to_send_kernel(x_ref, o_ref, came, put, in_sems, out_sems):
    shift = row_shift()
    group = 2 * PAIRS // PIECES
    for g in range(PIECES):
        part = pl.ds(g * group, group)
        pltpu.make_async_copy(x_ref.at[:, part], came.at[:, part], in_sems.at[g]).start()
    rows = came.reshape(2 * PAIRS * NMEM, PV)
    copies = []
    for g in range(PIECES):
        part = pl.ds(g * group, group)
        pltpu.make_async_copy(x_ref.at[:, part], came.at[:, part], in_sems.at[g]).wait()
        for chip in range(g * group // 4, (g + 1) * group // 4):
            for patch in range(4 * chip, 4 * chip + 4):
                put[sent_row(patch, shift)] = rows[pl.ds(patch, NMEM, stride=2 * PAIRS), :]
            part = pl.ds(sent_row(4 * chip, shift), 4)
            copies.append(pltpu.make_async_copy(put.at[part], o_ref.at[part], out_sems.at[chip]))
            copies[-1].start()
    for copy in copies:
        copy.wait()


def from_sent_kernel(x_ref, o_ref, put, sems):
    shift = row_shift()
    step = NMEM // PIECES
    copies = []
    for g in range(PIECES):
        first = g * step * 2 * PAIRS
        for patch in range(2 * PAIRS):
            put[pl.ds(first + patch, step, stride=2 * PAIRS), :] = x_ref[
                sent_row(patch, shift), g * step : (g + 1) * step
            ]
        part = pl.ds(first, step * 2 * PAIRS)
        copies.append(pltpu.make_async_copy(put.at[part], o_ref.at[part], sems.at[g]))
        copies[-1].start()
    for copy in copies:
        copy.wait()


def forecast_kernel(x_ref, g_ref, wi_ref, bi_ref, wo_ref, bo_ref, o_ref, wi2, wo2):
    for both, one in ((wi2, (wi_ref[...].astype(F32) * 0.5).astype(BF16)), (wo2, wo_ref[...])):
        zero = jnp.zeros_like(one)
        both[:LEV, :HID] = one
        both[:LEV, HID:] = zero
        both[LEV:, :HID] = zero
        both[LEV:, HID:] = one
    gain = jnp.concatenate([g_ref[...]] * 2, axis=1)
    bi = jnp.concatenate([bi_ref[...]] * 2, axis=1) * 0.5
    bo = jnp.concatenate([bo_ref[...]] * 2, axis=1)
    row = lax.broadcasted_iota(jnp.int32, (2 * PV, PV), 0)
    col = lax.broadcasted_iota(jnp.int32, (2 * PV, PV), 1)
    halves = jnp.where((row % PV) // LEV == col // LEV, 1.0, 0.0).astype(BF16)
    chunk, shift = PAIRS, row_shift()
    for first in range(0, 2 * PAIRS, chunk):
        x = jnp.concatenate(
            [x_ref[pl.ds(first + i, NMEM, stride=2 * PAIRS), :] for i in range(chunk)], axis=0
        )
        for _ in range(HOPS):
            squares = jnp.concatenate(split(x * x), axis=1)
            inverse = lax.rsqrt(dot(squares, halves) * (1.0 / LEV) + 1e-6)
            normed = (x * inverse * gain).astype(BF16)
            h = dot(normed, wi2[...]) + bi
            hidden = (h + h * jnp.tanh(h)).astype(BF16)
            x = x + dot_t(hidden, wo2[...]) + bo
        for i in range(chunk):
            patch = first + i
            o_ref[sent_row(patch, shift)] = x[i * NMEM : (i + 1) * NMEM]


def exact(a, b):
    return jnp.dot(a, b, precision=lax.Precision.HIGHEST, preferred_element_type=F32)


def observe(x, slots):
    slots = jnp.broadcast_to(slots, x.shape)
    return jnp.take_along_axis(x, slots, axis=1, mode="promise_in_bounds")


def centred(x):
    return x - jnp.mean(x, axis=0, keepdims=True)


def identity():
    row = lax.broadcasted_iota(jnp.int32, (PV, PV), 0)
    return jnp.where(row == lax.broadcasted_iota(jnp.int32, (PV, PV), 1), 1.0, 0.0)


def inverses(matrices, s_ref, x_ref):
    deltas = []
    eye = identity()
    for j, s in enumerate(matrices):
        s2 = dot3(s, s)
        norms = jnp.sum(jnp.abs(s2), axis=0, keepdims=True)
        top = jnp.sqrt(jnp.max(norms, axis=1, keepdims=True))
        c = 2.0 / (top + 1.0)
        delta = (top - 1.0) / (top + 1.0)
        mu = 2.0 / (2.0 - delta * delta)
        x1 = (mu * c) * (2.0 * eye - c * s)
        t1 = (mu * c) * (2.0 * s - c * s2)
        delta = delta * delta / (2.0 - delta * delta)
        mu = 2.0 / (2.0 - delta * delta)
        s_ref[j] = s
        x_ref[j] = mu * (2.0 * x1 - dot3(x1, t1))
        deltas.append(jnp.max(delta * delta / (2.0 - delta * delta)))

    def more(state):
        return jnp.maximum(state[0], state[1]) > 0.02

    def sharpen(state):
        after = []
        for j in range(2):
            delta = state[j]
            x = x_ref[j]
            mu = 2.0 / (2.0 - delta * delta)
            x_ref[j] = mu * (2.0 * x - dot3(x, dot3(s_ref[j], x)))
            after.append(delta * delta / (2.0 - delta * delta))
        return tuple(after)

    lax.while_loop(more, sharpen, tuple(deltas))


def own_kernel(
    idx_ref, f_ref, p_ref, slot_ref, var_ref,
    ah, al, bh, bl, dh, dl, inv_ref, part_ref, base_ref, s_ref, x_ref,
):
    members = NMEM * NMEM
    root = lax.rsqrt(var_ref[...])
    for w in range(2):
        x = f_ref[:, w].reshape(members, PV)
        y = observe(x, slot_ref[w + 1 : w + 2, :])
        r = root[w + 1 : w + 2, :]
        ah[w], al[w] = split(centred(x))
        bh[w], bl[w] = split(centred(y) * r)
        dh[w], dl[w] = split((p_ref[:, w].reshape(members, PV) - y) * r)
    scale = 1.0 / (members - 1)
    matrices, crosses = [], []
    for j in range(2):
        o = idx_ref[j, 0] - 1
        high, low = bh[o], bl[o]
        mixed = tdot(high, low)
        matrices.append((tdot(high, high) + (mixed + mixed.T)) * scale + identity())
        crosses.append((tdot(high, ah[j]) + (tdot(high, al[j]) + tdot(low, ah[j]))) * scale)
    inverses(matrices, s_ref, x_ref)
    for j in range(2):
        s, x = s_ref[j], x_ref[j]
        x = 2.0 * x - dot3(x, dot3(s, x))
        x = 2.0 * x - exact(x, exact(s, x))
        inv_ref[j] = x
        part = exact(x, crosses[j])
        part_ref[j] = part
        o = idx_ref[j, 0] - 1
        ph, pl_ = split(part)
        gained = dot(dh[o], ph) + (dot(dh[o], pl_) + dot(dl[o], ph))
        base_ref[:, j] = f_ref[:, j] + gained.reshape(NMEM, NMEM, PV)


def update_kernel(
    idx_ref, f_ref, fl_ref, fr_ref, p_ref, pl_ref, pr_ref, slot_ref, var_ref,
    ah, al, bh, bl, dh, dl, inv_ref, part_ref, base_ref, o_ref, hh, hl, s_ref, x_ref,
):
    members = NMEM * NMEM
    scale = 1.0 / (members - 1)
    fields, readings = (fl_ref, fr_ref), (pl_ref, pr_ref)
    complements, crosses = [], []
    for j in range(2):
        o, h = idx_ref[j, 0] - 1, idx_ref[j, 1]
        apart = h == 3 * j
        x = jnp.where(apart, fields[j][...], f_ref[:, j]).reshape(members, PV)
        p = jnp.where(apart, readings[j][...], p_ref[:, j]).reshape(members, PV)
        y = observe(x, slot_ref[pl.ds(h, 1), :])
        r = lax.rsqrt(var_ref[pl.ds(h, 1), :])
        high, low = split(centred(y) * r)
        right = jnp.concatenate([bh[o], high, ah[j]], axis=1)
        under = jnp.concatenate([bl[o], low, al[j]], axis=1)
        gram = (tdot(high, right) + (tdot(high, under) + tdot(low, right))) * scale
        s_ho, s_hh, g_h = gram[:, :PV], gram[:, PV : 2 * PV] + identity(), gram[:, 2 * PV :]
        link = dot3(s_ho, inv_ref[j])
        complements.append(s_hh - dot3(link, s_ho.T))
        crosses.append(g_h - dot3(s_ho, part_ref[j]))
        lh, ll = split(link)
        carried = dot_t(dh[o], lh) + (dot_t(dh[o], ll) + dot_t(dl[o], lh))
        hh[j], hl[j] = split((p - y) * r - carried)
    inverses(complements, s_ref, x_ref)
    for j in range(2):
        s, x, g = s_ref[j], x_ref[j], crosses[j]
        k_h = dot3(x, g)
        for _ in range(2):
            k_h = k_h + dot3(x, g - exact(s, k_h))
        kh, kl = split(k_h)
        gained = dot(hh[j], kh) + (dot(hh[j], kl) + dot(hl[j], kh))
        o_ref[:, j] = base_ref[:, j] + gained.reshape(NMEM, NMEM, PV)


def copying_call(kernel, out, space, scratch, limit=16):
    return pl.pallas_call(
        kernel,
        out_shape=jax.ShapeDtypeStruct(out, F32),
        in_specs=[pl.BlockSpec(memory_space=space)],
        out_specs=pl.BlockSpec(memory_space=pl.ANY),
        scratch_shapes=scratch,
        compiler_params=pltpu.CompilerParams(vmem_limit_bytes=limit << 20),
        cost_estimate=pl.CostEstimate(flops=10**9, bytes_accessed=2 << 20, transcendentals=0),
    )


def vmem_call(kernel, out, scratch=(), smem=0, limit=24, n_in=1, us=2):
    specs = [pl.BlockSpec(memory_space=pltpu.SMEM)] * smem
    specs += [pl.BlockSpec(memory_space=pltpu.VMEM)] * (n_in - smem)
    single = isinstance(out, tuple)
    shapes = jax.ShapeDtypeStruct(out, F32) if single else out
    return pl.pallas_call(
        kernel,
        out_shape=shapes,
        in_specs=specs,
        out_specs=jax.tree.map(lambda _: pl.BlockSpec(memory_space=pltpu.VMEM), shapes),
        scratch_shapes=list(scratch),
        compiler_params=pltpu.CompilerParams(vmem_limit_bytes=limit << 20),
        cost_estimate=pl.CostEstimate(
            flops=us * 10**9, bytes_accessed=1 << 20, transcendentals=0
        ),
    )


def body(
    prior_sample_set, perturbed_obs, measured_slot_table, obs_var, neighbours,
    norm_gain, w_in, b_in, w_out, b_out,
):
    rows = 2 * PAIRS * NMEM
    sent = (2 * PAIRS, NMEM, PV)
    packed = (NMEM, 2, NMEM, PV)
    both = ("mem", "space")
    first = 2 * pair_of(lax.axis_index("mem"), lax.axis_index("space"))

    pert_send = copying_call(
        to_send_kernel, sent, pl.ANY,
        [
            pltpu.VMEM(perturbed_obs.shape, F32), pltpu.VMEM(sent, F32),
            pltpu.SemaphoreType.DMA((PIECES,)), pltpu.SemaphoreType.DMA((PAIRS // 2,)),
        ],
        limit=60,
    )(perturbed_obs)
    pert = lax.all_to_all(pert_send.reshape(packed), "mem", 0, 0, tiled=True)

    field_send = vmem_call(
        forecast_kernel, sent,
        [pltpu.VMEM((2 * LEV, 2 * HID), BF16)] * 2, n_in=6, us=7,
    )(
        prior_sample_set.reshape(rows, PV), norm_gain.reshape(1, -1), w_in, b_in.reshape(1, -1),
        w_out.T, b_out.reshape(1, -1),
    )
    meta = jnp.concatenate([measured_slot_table.astype(F32), obs_var], axis=-1)
    field_send, meta = lax.optimization_barrier((field_send, meta))
    field = lax.all_to_all(field_send.reshape(packed), "mem", 0, 0, tiled=True)

    runs = [(i, (i + 1) % 8) for i in range(8)]
    before = lax.ppermute(meta[-1:], "space", runs)
    after = lax.ppermute(meta[:1], "space", [(j, i) for i, j in runs])
    window = lax.dynamic_slice_in_dim(
        jnp.concatenate([before, meta, after], axis=0), first, 4, 0
    )
    slots, variances = window[:, :PV].astype(jnp.int32), window[:, PV:]
    named = lax.dynamic_slice_in_dim(neighbours, first, 2, 0)
    own = jnp.arange(2, dtype=jnp.int32)[:, None]
    place = lax.axis_index("space") * (2 * PAIRS) + first + own
    index = (named - place + 1) % 512 + own

    rightward, leftward = neighbour_moves(1), neighbour_moves(-1)
    pert_left = lax.ppermute(pert[:, 1], both, rightward)
    pert_right = lax.ppermute(pert[:, 0], both, leftward)
    field_left = lax.ppermute(field[:, 1], both, rightward)
    field_right = lax.ppermute(field[:, 0], both, leftward)

    members = NMEM * NMEM
    pair = jax.ShapeDtypeStruct((2, members, PV), BF16)
    small = jax.ShapeDtypeStruct((2, PV, PV), F32)
    base = jax.ShapeDtypeStruct(packed, F32)
    half = pltpu.VMEM((2, members, PV), BF16)
    square = pltpu.VMEM((2, PV, PV), F32)
    index = jnp.concatenate([index[:1, ::-1], index[1:]], axis=0)
    own_parts = vmem_call(
        own_kernel, [pair] * 6 + [small] * 2 + [base], [square, square], smem=1, n_in=5, us=9
    )(index, field, pert, slots, variances)
    analysis = vmem_call(update_kernel, packed, [half, half, square, square], smem=1, n_in=18, us=7)(
        index, field, field_left, field_right, pert, pert_left, pert_right, slots, variances,
        *own_parts,
    )
    returned = lax.all_to_all(analysis, "mem", 0, 0, tiled=True)
    out = copying_call(
        from_sent_kernel, (rows, PV), pltpu.VMEM,
        [pltpu.VMEM((rows, PV), F32), pltpu.SemaphoreType.DMA((PIECES,))],
    )(returned.reshape(sent))
    return out.reshape(prior_sample_set.shape)


def solution(mesh):
    rows = P("space", None)
    cube = P("mem", "space", None)
    return jax.shard_map(
        body,
        mesh=mesh,
        in_specs=(cube, cube, rows, rows, rows, P(), P(), P(), P(), P()),
        out_specs=cube,
        check_vma=False,
    )
```

```python
import jax
import jax.numpy as jnp
from jax import lax
from jax.experimental import pallas as pl
from jax.experimental.pallas import tpu as pltpu
from jax.sharding import PartitionSpec as P

LEV = 64
HID = 512
HOPS = 2
PV = 128
NMEM = 32
PIECES = 4
WIDE = 100.0
PAIRS = 32
F32 = jnp.float32
BF16 = jnp.bfloat16


def owner_of(pair):
    chip, core = pair // 2, pair % 2
    z, x = (chip, 0) if chip < 8 else (15 - chip, 1)
    return (z * 2 + x) * 2 + core


def mirrored(run):
    return (run + 1 + run // 4) % 2


def pair_of(member, run):
    z, x, core = member // 4, (member // 2 + mirrored(run)) % 2, member % 2
    return 2 * jnp.where(x == 0, z, 15 - z) + core


def neighbour_moves(step):
    runs = 8

    def device(patches):
        run, pair = patches // PAIRS % runs, patches % PAIRS
        return (owner_of(pair) ^ 2 * mirrored(run)) * runs + run

    return [(device(here), device(here + step)) for here in range(runs * PAIRS)]


def dot(a, b):
    return jnp.dot(a, b, preferred_element_type=F32)


def dot_t(a, b):
    return lax.dot_general(a, b, (((1,), (1,)), ((), ())), preferred_element_type=F32)


def tdot(a, b):
    return lax.dot_general(a, b, (((0,), (0,)), ((), ())), preferred_element_type=F32)


def split(a):
    high = a.astype(BF16)
    return high, (a - high.astype(F32)).astype(BF16)


def dot3(a, b):
    (ah, al), (bh, bl) = split(a), split(b)
    return dot(ah, bh) + (dot(ah, bl) + dot(al, bh))


def row_shift():
    return 4 * mirrored(lax.axis_index("space"))


def sent_row(patch, shift):
    row = 2 * owner_of(patch // 2) + patch % 2
    return row - shift if row & 4 else row + shift


def to_send_kernel(x_ref, o_ref, came, put, in_sems, out_sems):
    shift = row_shift()
    group = 2 * PAIRS // PIECES
    for g in range(PIECES):
        part = pl.ds(g * group, group)
        pltpu.make_async_copy(x_ref.at[:, part], came.at[:, part], in_sems.at[g]).start()
    rows = came.reshape(2 * PAIRS * NMEM, PV)
    copies = []
    for g in range(PIECES):
        part = pl.ds(g * group, group)
        pltpu.make_async_copy(x_ref.at[:, part], came.at[:, part], in_sems.at[g]).wait()
        for chip in range(g * group // 4, (g + 1) * group // 4):
            for patch in range(4 * chip, 4 * chip + 4):
                put[sent_row(patch, shift)] = rows[pl.ds(patch, NMEM, stride=2 * PAIRS), :]
            part = pl.ds(sent_row(4 * chip, shift), 4)
            copies.append(pltpu.make_async_copy(put.at[part], o_ref.at[part], out_sems.at[chip]))
            copies[-1].start()
    for copy in copies:
        copy.wait()


def from_sent_kernel(x_ref, o_ref, put, sems):
    shift = row_shift()
    step = NMEM // PIECES
    copies = []
    for g in range(PIECES):
        first = g * step * 2 * PAIRS
        for patch in range(2 * PAIRS):
            put[pl.ds(first + patch, step, stride=2 * PAIRS), :] = x_ref[
                sent_row(patch, shift), g * step : (g + 1) * step
            ]
        part = pl.ds(first, step * 2 * PAIRS)
        copies.append(pltpu.make_async_copy(put.at[part], o_ref.at[part], sems.at[g]))
        copies[-1].start()
    for copy in copies:
        copy.wait()


def forecast_kernel(x_ref, g_ref, wi_ref, bi_ref, wo_ref, bo_ref, o_ref, wi2, wo2):
    for both, one in ((wi2, (wi_ref[...].astype(F32) * 0.5).astype(BF16)), (wo2, wo_ref[...])):
        zero = jnp.zeros_like(one)
        both[:LEV, :HID] = one
        both[:LEV, HID:] = zero
        both[LEV:, :HID] = zero
        both[LEV:, HID:] = one
    gain = jnp.concatenate([g_ref[...]] * 2, axis=1)
    bi = jnp.concatenate([bi_ref[...]] * 2, axis=1) * 0.5
    bo = jnp.concatenate([bo_ref[...]] * 2, axis=1)
    row = lax.broadcasted_iota(jnp.int32, (2 * PV, PV), 0)
    col = lax.broadcasted_iota(jnp.int32, (2 * PV, PV), 1)
    halves = jnp.where((row % PV) // LEV == col // LEV, 1.0, 0.0).astype(BF16)
    chunk, shift = PAIRS, row_shift()
    for first in range(0, 2 * PAIRS, chunk):
        x = jnp.concatenate(
            [x_ref[pl.ds(first + i, NMEM, stride=2 * PAIRS), :] for i in range(chunk)], axis=0
        )
        for _ in range(HOPS):
            squares = jnp.concatenate(split(x * x), axis=1)
            inverse = lax.rsqrt(dot(squares, halves) * (1.0 / LEV) + 1e-6)
            normed = (x * inverse * gain).astype(BF16)
            h = dot(normed, wi2[...]) + bi
            hidden = (h + h * jnp.tanh(h)).astype(BF16)
            x = x + dot_t(hidden, wo2[...]) + bo
        for i in range(chunk):
            patch = first + i
            o_ref[sent_row(patch, shift)] = x[i * NMEM : (i + 1) * NMEM]


def exact(a, b):
    return jnp.dot(a, b, precision=lax.Precision.HIGHEST, preferred_element_type=F32)


def observe(x, slots):
    slots = jnp.broadcast_to(slots, x.shape)
    return jnp.take_along_axis(x, slots, axis=1, mode="promise_in_bounds")


def centred(x):
    return x - jnp.mean(x, axis=0, keepdims=True)


def identity():
    row = lax.broadcasted_iota(jnp.int32, (PV, PV), 0)
    return jnp.where(row == lax.broadcasted_iota(jnp.int32, (PV, PV), 1), 1.0, 0.0)


def closer(delta):
    return delta * delta / (2.0 - delta * delta)


def sharper(s, x, delta, product=dot3):
    return (2.0 / (2.0 - delta * delta)) * (2.0 * x - product(x, product(s, x)))


def inverses(matrices, s_ref, x_ref, steps, goal):
    eye = identity()
    xs, deltas, tops = [], [], []
    for s in matrices:
        s2 = dot3(s, s)
        norms = jnp.sum(jnp.abs(s2), axis=0, keepdims=True)
        top = jnp.sqrt(jnp.max(norms, axis=1, keepdims=True))
        c = 2.0 / (top + 1.0)
        delta = (top - 1.0) / (top + 1.0)
        mu = 2.0 / (2.0 - delta * delta)
        x1 = (mu * c) * (2.0 * eye - c * s)
        t1 = (mu * c) * (2.0 * s - c * s2)
        delta = closer(delta)
        xs.append((2.0 / (2.0 - delta * delta)) * (2.0 * x1 - dot3(x1, t1)))
        deltas.append(closer(delta))
        tops.append(jnp.max(top))
    for _ in range(steps):
        xs = [sharper(*it) for it in zip(matrices, xs, deltas)]
        deltas = [closer(delta) for delta in deltas]
    for j in range(2):
        s_ref[j] = matrices[j]
        x_ref[j] = xs[j]

    def more(state):
        return jnp.maximum(state[0], state[1]) > goal

    def sharpen(state):
        for j in range(2):
            x_ref[j] = sharper(s_ref[j], x_ref[j], state[j])
        return tuple(closer(delta) for delta in state)

    last = lax.while_loop(more, sharpen, tuple(jnp.max(delta) for delta in deltas))

    @pl.when(jnp.maximum(*tops) > WIDE)
    def _():
        for j in range(2):
            x_ref[j] = (2.0 / (tops[j] + 1.0)) * eye

            def once(delta, j=j):
                x_ref[j] = sharper(s_ref[j], x_ref[j], delta, exact)
                return closer(delta)

            start = (tops[j] - 1.0) / (tops[j] + 1.0)
            lax.while_loop(lambda delta: delta > 1e-4, once, once(start))
            x_ref[j] = 2.0 * x_ref[j] - exact(x_ref[j], exact(s_ref[j], x_ref[j]))

    return jnp.maximum(*last), jnp.maximum(*tops)


def own_kernel(
    idx_ref, f_ref, p_ref, slot_ref, var_ref,
    ah, al, bh, bl, dh, dl, inv_ref, part_ref, base_ref, s_ref, x_ref,
):
    members = NMEM * NMEM
    root = lax.rsqrt(var_ref[...])
    for w in range(2):
        x = f_ref[:, w].reshape(members, PV)
        y = observe(x, slot_ref[w + 1 : w + 2, :])
        r = root[w + 1 : w + 2, :]
        ah[w], al[w] = split(centred(x))
        bh[w], bl[w] = split(centred(y) * r)
        dh[w], dl[w] = split((p_ref[:, w].reshape(members, PV) - y) * r)
    scale = 1.0 / (members - 1)
    matrices, crosses = [], []
    for j in range(2):
        o = idx_ref[j, 0] - 1
        high, low = bh[o], bl[o]
        mixed = tdot(high, low)
        small = mixed + (mixed.T + tdot(low, low))
        matrices.append((tdot(high, high) + small) * scale + identity())
        small = tdot(high, al[j]) + (tdot(low, ah[j]) + tdot(low, al[j]))
        crosses.append((tdot(high, ah[j]) + small) * scale)
    inverses(matrices, s_ref, x_ref, 3, 1e-4)
    for j in range(2):
        x = x_ref[j]
        inv_ref[j] = x
        part = exact(x, crosses[j])
        part_ref[j] = part
        o = idx_ref[j, 0] - 1
        ph, pl_ = split(part)
        gained = dot(dh[o], ph) + (dot(dh[o], pl_) + dot(dl[o], ph))
        base_ref[:, j] = f_ref[:, j] + gained.reshape(NMEM, NMEM, PV)


def update_kernel(
    idx_ref, f_ref, fl_ref, fr_ref, p_ref, pl_ref, pr_ref, slot_ref, var_ref,
    ah, al, bh, bl, dh, dl, inv_ref, part_ref, base_ref, o_ref, hh, hl, s_ref, x_ref,
    g_ref, k_ref, link_ref, gram_ref, d_ref,
):
    members = NMEM * NMEM
    scale = 1.0 / (members - 1)
    fields, readings = (fl_ref, fr_ref), (pl_ref, pr_ref)
    norms = []
    for j in range(2):
        o, h = idx_ref[j, 0] - 1, idx_ref[j, 1]
        apart = h == 3 * j
        x = jnp.where(apart, fields[j][...], f_ref[:, j]).reshape(members, PV)
        p = jnp.where(apart, readings[j][...], p_ref[:, j]).reshape(members, PV)
        y = observe(x, slot_ref[pl.ds(h, 1), :])
        r = lax.rsqrt(var_ref[pl.ds(h, 1), :])
        high, low = split(centred(y) * r)
        d_ref[j] = (p - y) * r
        right = jnp.concatenate([bh[o], high, ah[j]], axis=1)
        under = jnp.concatenate([bl[o], low, al[j]], axis=1)
        small = tdot(high, under) + (tdot(low, right) + tdot(low, under))
        gram = (tdot(high, right) + small) * scale
        gram_ref[j] = gram
        norms.append(jnp.sum(gram * gram))

    def eliminate(j, product):
        s_ho, s_hh, g_h = (gram_ref[j, :, n * PV : (n + 1) * PV] for n in range(3))
        link = product(s_ho, inv_ref[j])
        link_ref[j] = link
        s_ref[j] = s_hh + identity() - product(link, s_ho.T)
        g_ref[j] = g_h - product(s_ho, part_ref[j])

    for j in range(2):
        eliminate(j, dot3)

    @pl.when(jnp.maximum(*norms) > 300.0**2)
    def _():
        for j in range(2):
            eliminate(j, exact)

    for j in range(2):
        o = idx_ref[j, 0] - 1
        lh, ll = split(link_ref[j])
        carried = dot_t(dh[o], lh) + (dot_t(dh[o], ll) + dot_t(dl[o], lh))
        hh[j], hl[j] = split(d_ref[j] - carried)
    complements = [s_ref[j] for j in range(2)]
    delta, top = inverses(complements, s_ref, x_ref, 2, 0.01)
    for j in range(2):
        s, x, g = s_ref[j], x_ref[j], g_ref[j]
        k = dot3(x, g)
        k_ref[j] = k + dot3(x, g - dot3(s, k))

    @pl.when(jnp.maximum(delta * (WIDE / 0.0055), top) > WIDE)
    def _():
        for j in range(2):
            for _ in range(2):
                k_ref[j] += dot3(x_ref[j], g_ref[j] - exact(s_ref[j], k_ref[j]))

    for j in range(2):
        kh, kl = split(k_ref[j])
        gained = dot(hh[j], kh) + (dot(hh[j], kl) + dot(hl[j], kh))
        o_ref[:, j] = base_ref[:, j] + gained.reshape(NMEM, NMEM, PV)


def copying_call(kernel, out, space, scratch, limit=16):
    return pl.pallas_call(
        kernel,
        out_shape=jax.ShapeDtypeStruct(out, F32),
        in_specs=[pl.BlockSpec(memory_space=space)],
        out_specs=pl.BlockSpec(memory_space=pl.ANY),
        scratch_shapes=scratch,
        compiler_params=pltpu.CompilerParams(vmem_limit_bytes=limit << 20),
        cost_estimate=pl.CostEstimate(flops=10**9, bytes_accessed=2 << 20, transcendentals=0),
    )


def vmem_call(kernel, out, scratch=(), smem=0, limit=24, n_in=1, us=2):
    specs = [pl.BlockSpec(memory_space=pltpu.SMEM)] * smem
    specs += [pl.BlockSpec(memory_space=pltpu.VMEM)] * (n_in - smem)
    single = isinstance(out, tuple)
    shapes = jax.ShapeDtypeStruct(out, F32) if single else out
    return pl.pallas_call(
        kernel,
        out_shape=shapes,
        in_specs=specs,
        out_specs=jax.tree.map(lambda _: pl.BlockSpec(memory_space=pltpu.VMEM), shapes),
        scratch_shapes=list(scratch),
        compiler_params=pltpu.CompilerParams(vmem_limit_bytes=limit << 20),
        cost_estimate=pl.CostEstimate(
            flops=us * 10**9, bytes_accessed=1 << 20, transcendentals=0
        ),
    )


def body(
    prior_sample_set, perturbed_obs, measured_slot_table, obs_var, neighbours,
    norm_gain, w_in, b_in, w_out, b_out,
):
    rows = 2 * PAIRS * NMEM
    sent = (2 * PAIRS, NMEM, PV)
    packed = (NMEM, 2, NMEM, PV)
    both = ("mem", "space")
    first = 2 * pair_of(lax.axis_index("mem"), lax.axis_index("space"))

    pert_send = copying_call(
        to_send_kernel, sent, pl.ANY,
        [
            pltpu.VMEM(perturbed_obs.shape, F32), pltpu.VMEM(sent, F32),
            pltpu.SemaphoreType.DMA((PIECES,)), pltpu.SemaphoreType.DMA((PAIRS // 2,)),
        ],
        limit=60,
    )(perturbed_obs)
    pert = lax.all_to_all(pert_send.reshape(packed), "mem", 0, 0, tiled=True)

    field_send = vmem_call(
        forecast_kernel, sent,
        [pltpu.VMEM((2 * LEV, 2 * HID), BF16)] * 2, n_in=6, us=7,
    )(
        prior_sample_set.reshape(rows, PV), norm_gain.reshape(1, -1), w_in, b_in.reshape(1, -1),
        w_out.T, b_out.reshape(1, -1),
    )
    meta = jnp.concatenate([measured_slot_table.astype(F32), obs_var], axis=-1)
    field_send, meta = lax.optimization_barrier((field_send, meta))
    field = lax.all_to_all(field_send.reshape(packed), "mem", 0, 0, tiled=True)

    runs = [(i, (i + 1) % 8) for i in range(8)]
    before = lax.ppermute(meta[-1:], "space", runs)
    after = lax.ppermute(meta[:1], "space", [(j, i) for i, j in runs])
    window = lax.dynamic_slice_in_dim(
        jnp.concatenate([before, meta, after], axis=0), first, 4, 0
    )
    slots, variances = window[:, :PV].astype(jnp.int32), window[:, PV:]
    named = lax.dynamic_slice_in_dim(neighbours, first, 2, 0)
    own = jnp.arange(2, dtype=jnp.int32)[:, None]
    place = lax.axis_index("space") * (2 * PAIRS) + first + own
    index = (named - place + 1) % 512 + own

    rightward, leftward = neighbour_moves(1), neighbour_moves(-1)
    pert_left = lax.ppermute(pert[:, 1], both, rightward)
    pert_right = lax.ppermute(pert[:, 0], both, leftward)
    field_left = lax.ppermute(field[:, 1], both, rightward)
    field_right = lax.ppermute(field[:, 0], both, leftward)

    members = NMEM * NMEM
    pair = jax.ShapeDtypeStruct((2, members, PV), BF16)
    small = jax.ShapeDtypeStruct((2, PV, PV), F32)
    base = jax.ShapeDtypeStruct(packed, F32)
    half = pltpu.VMEM((2, members, PV), BF16)
    square = pltpu.VMEM((2, PV, PV), F32)
    scratch = [half, half] + [square] * 5
    scratch += [pltpu.VMEM((2, PV, 3 * PV), F32), pltpu.VMEM((2, members, PV), F32)]
    index = jnp.concatenate([index[:1, ::-1], index[1:]], axis=0)
    own_parts = vmem_call(
        own_kernel, [pair] * 6 + [small] * 2 + [base], [square, square], smem=1, n_in=5, us=9
    )(index, field, pert, slots, variances)
    analysis = vmem_call(update_kernel, packed, scratch, smem=1, n_in=18, us=7)(
        index, field, field_left, field_right, pert, pert_left, pert_right, slots, variances,
        *own_parts,
    )
    returned = lax.all_to_all(analysis, "mem", 0, 0, tiled=True)
    out = copying_call(
        from_sent_kernel, (rows, PV), pltpu.VMEM,
        [pltpu.VMEM((rows, PV), F32), pltpu.SemaphoreType.DMA((PIECES,))],
    )(returned.reshape(sent))
    return out.reshape(prior_sample_set.shape)


def solution(mesh):
    rows = P("space", None)
    cube = P("mem", "space", None)
    return jax.shard_map(
        body,
        mesh=mesh,
        in_specs=(cube, cube, rows, rows, rows, P(), P(), P(), P(), P()),
        out_specs=cube,
        check_vma=False,
    )
```

```python
import jax
import jax.numpy as jnp
from jax import lax
from jax.experimental import pallas as pl
from jax.experimental.pallas import tpu as pltpu
from jax.sharding import PartitionSpec as P

LEV = 64
HID = 512
HOPS = 2
PV = 128
NMEM = 32
PIECES = 4
WIDE = 100.0
PAIRS = 32
F32 = jnp.float32
BF16 = jnp.bfloat16


def owner_of(pair):
    chip, core = pair // 2, pair % 2
    z, x = (chip, 0) if chip < 8 else (15 - chip, 1)
    return (z * 2 + x) * 2 + core


def mirrored(run):
    return (run + 1 + run // 4) % 2


def pair_of(member, run):
    z, x, core = member // 4, (member // 2 + mirrored(run)) % 2, member % 2
    return 2 * jnp.where(x == 0, z, 15 - z) + core


def neighbour_moves(step):
    runs = 8

    def device(patches):
        run, pair = patches // PAIRS % runs, patches % PAIRS
        return (owner_of(pair) ^ 2 * mirrored(run)) * runs + run

    return [(device(here), device(here + step)) for here in range(runs * PAIRS)]


def dot(a, b):
    return jnp.dot(a, b, preferred_element_type=F32)


def dot_t(a, b):
    return lax.dot_general(a, b, (((1,), (1,)), ((), ())), preferred_element_type=F32)


def split(a):
    high = a.astype(BF16)
    return high, (a - high.astype(F32)).astype(BF16)


def dot3(a, b):
    (ah, al), (bh, bl) = split(a), split(b)
    return dot(ah, bh) + (dot(ah, bl) + dot(al, bh))


def row_shift():
    return 4 * mirrored(lax.axis_index("space"))


def sent_row(patch, shift):
    row = 2 * owner_of(patch // 2) + patch % 2
    return row - shift if row & 4 else row + shift


def to_send_kernel(x_ref, o_ref, came, put, in_sems, out_sems):
    shift = row_shift()
    group = 2 * PAIRS // PIECES
    for g in range(PIECES):
        part = pl.ds(g * group, group)
        pltpu.make_async_copy(x_ref.at[:, part], came.at[:, part], in_sems.at[g]).start()
    rows = came.reshape(2 * PAIRS * NMEM, PV)
    copies = []
    for g in range(PIECES):
        part = pl.ds(g * group, group)
        pltpu.make_async_copy(x_ref.at[:, part], came.at[:, part], in_sems.at[g]).wait()
        for chip in range(g * group // 4, (g + 1) * group // 4):
            for patch in range(4 * chip, 4 * chip + 4):
                put[sent_row(patch, shift)] = rows[pl.ds(patch, NMEM, stride=2 * PAIRS), :]
            part = pl.ds(sent_row(4 * chip, shift), 4)
            copies.append(pltpu.make_async_copy(put.at[part], o_ref.at[part], out_sems.at[chip]))
            copies[-1].start()
    for copy in copies:
        copy.wait()


def from_sent_kernel(x_ref, o_ref, put, sems):
    shift = row_shift()
    step = NMEM // PIECES
    copies = []
    for g in range(PIECES):
        first = g * step * 2 * PAIRS
        for patch in range(2 * PAIRS):
            put[pl.ds(first + patch, step, stride=2 * PAIRS), :] = x_ref[
                sent_row(patch, shift), g * step : (g + 1) * step
            ]
        part = pl.ds(first, step * 2 * PAIRS)
        copies.append(pltpu.make_async_copy(put.at[part], o_ref.at[part], sems.at[g]))
        copies[-1].start()
    for copy in copies:
        copy.wait()


def forecast_kernel(x_ref, g_ref, wi_ref, bi_ref, wo_ref, bo_ref, o_ref, wi2, wo2):
    for both, one in ((wi2, (wi_ref[...].astype(F32) * 0.5).astype(BF16)), (wo2, wo_ref[...])):
        zero = jnp.zeros_like(one)
        both[:LEV, :HID] = one
        both[:LEV, HID:] = zero
        both[LEV:, :HID] = zero
        both[LEV:, HID:] = one
    gain = jnp.concatenate([g_ref[...]] * 2, axis=1)
    bi = jnp.concatenate([bi_ref[...]] * 2, axis=1) * 0.5
    bo = jnp.concatenate([bo_ref[...]] * 2, axis=1)
    row = lax.broadcasted_iota(jnp.int32, (2 * PV, PV), 0)
    col = lax.broadcasted_iota(jnp.int32, (2 * PV, PV), 1)
    halves = jnp.where((row % PV) // LEV == col // LEV, 1.0, 0.0).astype(BF16)
    chunk, shift = PAIRS, row_shift()
    for first in range(0, 2 * PAIRS, chunk):
        x = jnp.concatenate(
            [x_ref[pl.ds(first + i, NMEM, stride=2 * PAIRS), :] for i in range(chunk)], axis=0
        )
        for _ in range(HOPS):
            squares = jnp.concatenate(split(x * x), axis=1)
            inverse = lax.rsqrt(dot(squares, halves) * (1.0 / LEV) + 1e-6)
            normed = (x * inverse * gain).astype(BF16)
            h = dot(normed, wi2[...]) + bi
            hidden = (h + h * jnp.tanh(h)).astype(BF16)
            x = x + dot_t(hidden, wo2[...]) + bo
        for i in range(chunk):
            patch = first + i
            o_ref[sent_row(patch, shift)] = x[i * NMEM : (i + 1) * NMEM]


def exact(a, b):
    return jnp.dot(a, b, precision=lax.Precision.HIGHEST, preferred_element_type=F32)


def observe(x, slots):
    slots = jnp.broadcast_to(slots, x.shape)
    return jnp.take_along_axis(x, slots, axis=1, mode="promise_in_bounds")


def centred(x):
    return x - jnp.mean(x, axis=0, keepdims=True)


def identity():
    row = lax.broadcasted_iota(jnp.int32, (PV, PV), 0)
    return jnp.where(row == lax.broadcasted_iota(jnp.int32, (PV, PV), 1), 1.0, 0.0)


def closer(delta):
    return delta * delta / (2.0 - delta * delta)


def sharper(s, x, delta, product=dot3):
    return (2.0 / (2.0 - delta * delta)) * (2.0 * x - product(x, product(s, x)))


def inverses(matrices, s_ref, x_ref, steps, goal):
    eye = identity()
    xs, deltas, tops = [], [], []
    for s in matrices:
        s2 = dot3(s, s)
        norms = jnp.sum(jnp.abs(s2), axis=0, keepdims=True)
        top = jnp.sqrt(jnp.max(norms, axis=1, keepdims=True))
        c = 2.0 / (top + 1.0)
        delta = (top - 1.0) / (top + 1.0)
        mu = 2.0 / (2.0 - delta * delta)
        x1 = (mu * c) * (2.0 * eye - c * s)
        t1 = (mu * c) * (2.0 * s - c * s2)
        delta = closer(delta)
        xs.append((2.0 / (2.0 - delta * delta)) * (2.0 * x1 - dot3(x1, t1)))
        deltas.append(closer(delta))
        tops.append(jnp.max(top))
    for _ in range(steps):
        xs = [sharper(*it) for it in zip(matrices, xs, deltas)]
        deltas = [closer(delta) for delta in deltas]
    for j in range(2):
        s_ref[j] = matrices[j]
        x_ref[j] = xs[j]

    def more(state):
        return jnp.maximum(state[0], state[1]) > goal

    def sharpen(state):
        for j in range(2):
            x_ref[j] = sharper(s_ref[j], x_ref[j], state[j])
        return tuple(closer(delta) for delta in state)

    last = lax.while_loop(more, sharpen, tuple(jnp.max(delta) for delta in deltas))

    @pl.when(jnp.maximum(*tops) > WIDE)
    def _():
        for j in range(2):
            x_ref[j] = (2.0 / (tops[j] + 1.0)) * eye

            def once(delta, j=j):
                x_ref[j] = sharper(s_ref[j], x_ref[j], delta, exact)
                return closer(delta)

            start = (tops[j] - 1.0) / (tops[j] + 1.0)
            lax.while_loop(lambda delta: delta > 1e-4, once, once(start))
            x_ref[j] = 2.0 * x_ref[j] - exact(x_ref[j], exact(s_ref[j], x_ref[j]))

    return jnp.maximum(*last), jnp.maximum(*tops)


def own_kernel(
    idx_ref, f_ref, p_ref, slot_ref, var_ref,
    ath, atl, bth, btl, dh, dl, inv_ref, part_ref, base_ref, ah, al, bh, bl, s_ref, x_ref,
):
    members = NMEM * NMEM
    root = lax.rsqrt(var_ref[...])
    for w in range(2):
        x = f_ref[:, w].reshape(members, PV)
        y = observe(x, slot_ref[w + 1 : w + 2, :])
        r = root[w + 1 : w + 2, :]
        a, b = centred(x), centred(y) * r
        ah[w], al[w] = split(a)
        bh[w], bl[w] = split(b)
        ath[w], atl[w] = split(a.T)
        bth[w], btl[w] = split(b.T)
        dh[w], dl[w] = split((p_ref[:, w].reshape(members, PV) - y) * r)
    scale = 1.0 / (members - 1)
    matrices, crosses = [], []
    for j in range(2):
        o = idx_ref[j, 0] - 1
        high, low = bth[o], btl[o]
        mixed = dot(high, bl[o])
        small = mixed + (mixed.T + dot(low, bl[o]))
        matrices.append((dot(high, bh[o]) + small) * scale + identity())
        small = dot(high, al[j]) + (dot(low, ah[j]) + dot(low, al[j]))
        crosses.append((dot(high, ah[j]) + small) * scale)
    inverses(matrices, s_ref, x_ref, 3, 1e-4)
    for j in range(2):
        x = x_ref[j]
        inv_ref[j] = x
        part = exact(x, crosses[j])
        part_ref[j] = part
        o = idx_ref[j, 0] - 1
        ph, pl_ = split(part)
        gained = dot(dh[o], ph) + (dot(dh[o], pl_) + dot(dl[o], ph))
        base_ref[:, j] = f_ref[:, j] + gained.reshape(NMEM, NMEM, PV)


def update_kernel(
    idx_ref, f_ref, fl_ref, fr_ref, p_ref, pl_ref, pr_ref, slot_ref, var_ref,
    ath, atl, bth, btl, dh, dl, inv_ref, part_ref, base_ref, o_ref, hh, hl, s_ref, x_ref,
    g_ref, k_ref, link_ref, gram_ref, d_ref,
):
    members = NMEM * NMEM
    scale = 1.0 / (members - 1)
    fields, readings = (fl_ref, fr_ref), (pl_ref, pr_ref)
    norms = []
    for j in range(2):
        o, h = idx_ref[j, 0] - 1, idx_ref[j, 1]
        apart = h == 3 * j
        x = jnp.where(apart, fields[j][...], f_ref[:, j]).reshape(members, PV)
        p = jnp.where(apart, readings[j][...], p_ref[:, j]).reshape(members, PV)
        y = observe(x, slot_ref[pl.ds(h, 1), :])
        r = lax.rsqrt(var_ref[pl.ds(h, 1), :])
        b = centred(y) * r
        d_ref[j] = (p - y) * r
        rows = [bth[o], btl[o], *split(b.T), ath[j], atl[j]]
        both = dot(jnp.concatenate(rows, axis=0), jnp.concatenate(split(b), axis=1))
        both = both[:, :PV] + both[:, PV:]
        s_oh, s_hh, g = (both[n : n + PV] + both[n + PV : n + 2 * PV] for n in (0, 2 * PV, 4 * PV))
        gram = jnp.concatenate([s_oh.T, s_hh, g.T], axis=1) * scale
        gram_ref[j] = gram
        norms.append(jnp.sum(gram * gram))

    def eliminate(j, product):
        s_ho, s_hh, g_h = (gram_ref[j, :, n * PV : (n + 1) * PV] for n in range(3))
        link = product(s_ho, inv_ref[j])
        link_ref[j] = link
        s_ref[j] = s_hh + identity() - product(link, s_ho.T)
        g_ref[j] = g_h - product(s_ho, part_ref[j])

    for j in range(2):
        eliminate(j, dot3)

    @pl.when(jnp.maximum(*norms) > 300.0**2)
    def _():
        for j in range(2):
            eliminate(j, exact)

    for j in range(2):
        o = idx_ref[j, 0] - 1
        lh, ll = split(link_ref[j])
        carried = dot_t(dh[o], lh) + (dot_t(dh[o], ll) + dot_t(dl[o], lh))
        hh[j], hl[j] = split(d_ref[j] - carried)
    complements = [s_ref[j] for j in range(2)]
    delta, top = inverses(complements, s_ref, x_ref, 2, 0.01)
    for j in range(2):
        s, x, g = s_ref[j], x_ref[j], g_ref[j]
        k = dot3(x, g)
        k_ref[j] = k + dot3(x, g - dot3(s, k))

    @pl.when(jnp.maximum(delta * (WIDE / 0.0055), top) > WIDE)
    def _():
        for j in range(2):
            for _ in range(2):
                k_ref[j] += dot3(x_ref[j], g_ref[j] - exact(s_ref[j], k_ref[j]))

    for j in range(2):
        kh, kl = split(k_ref[j])
        gained = dot(hh[j], kh) + (dot(hh[j], kl) + dot(hl[j], kh))
        o_ref[:, j] = base_ref[:, j] + gained.reshape(NMEM, NMEM, PV)


def copying_call(kernel, out, space, scratch, limit=16):
    return pl.pallas_call(
        kernel,
        out_shape=jax.ShapeDtypeStruct(out, F32),
        in_specs=[pl.BlockSpec(memory_space=space)],
        out_specs=pl.BlockSpec(memory_space=pl.ANY),
        scratch_shapes=scratch,
        compiler_params=pltpu.CompilerParams(vmem_limit_bytes=limit << 20),
        cost_estimate=pl.CostEstimate(flops=10**9, bytes_accessed=2 << 20, transcendentals=0),
    )


def vmem_call(kernel, out, scratch=(), smem=0, limit=24, n_in=1, us=2):
    specs = [pl.BlockSpec(memory_space=pltpu.SMEM)] * smem
    specs += [pl.BlockSpec(memory_space=pltpu.VMEM)] * (n_in - smem)
    single = isinstance(out, tuple)
    shapes = jax.ShapeDtypeStruct(out, F32) if single else out
    return pl.pallas_call(
        kernel,
        out_shape=shapes,
        in_specs=specs,
        out_specs=jax.tree.map(lambda _: pl.BlockSpec(memory_space=pltpu.VMEM), shapes),
        scratch_shapes=list(scratch),
        compiler_params=pltpu.CompilerParams(vmem_limit_bytes=limit << 20),
        cost_estimate=pl.CostEstimate(
            flops=us * 10**9, bytes_accessed=1 << 20, transcendentals=0
        ),
    )


def body(
    prior_sample_set, perturbed_obs, measured_slot_table, obs_var, neighbours,
    norm_gain, w_in, b_in, w_out, b_out,
):
    rows = 2 * PAIRS * NMEM
    sent = (2 * PAIRS, NMEM, PV)
    packed = (NMEM, 2, NMEM, PV)
    both = ("mem", "space")
    first = 2 * pair_of(lax.axis_index("mem"), lax.axis_index("space"))

    pert_send = copying_call(
        to_send_kernel, sent, pl.ANY,
        [
            pltpu.VMEM(perturbed_obs.shape, F32), pltpu.VMEM(sent, F32),
            pltpu.SemaphoreType.DMA((PIECES,)), pltpu.SemaphoreType.DMA((PAIRS // 2,)),
        ],
        limit=60,
    )(perturbed_obs)
    pert = lax.all_to_all(pert_send.reshape(packed), "mem", 0, 0, tiled=True)

    field_send = vmem_call(
        forecast_kernel, sent,
        [pltpu.VMEM((2 * LEV, 2 * HID), BF16)] * 2, n_in=6, us=7,
    )(
        prior_sample_set.reshape(rows, PV), norm_gain.reshape(1, -1), w_in, b_in.reshape(1, -1),
        w_out.T, b_out.reshape(1, -1),
    )
    meta = jnp.concatenate([measured_slot_table.astype(F32), obs_var], axis=-1)
    field_send, meta = lax.optimization_barrier((field_send, meta))
    field = lax.all_to_all(field_send.reshape(packed), "mem", 0, 0, tiled=True)

    runs = [(i, (i + 1) % 8) for i in range(8)]
    before = lax.ppermute(meta[-1:], "space", runs)
    after = lax.ppermute(meta[:1], "space", [(j, i) for i, j in runs])
    window = lax.dynamic_slice_in_dim(
        jnp.concatenate([before, meta, after], axis=0), first, 4, 0
    )
    slots, variances = window[:, :PV].astype(jnp.int32), window[:, PV:]
    named = lax.dynamic_slice_in_dim(neighbours, first, 2, 0)
    own = jnp.arange(2, dtype=jnp.int32)[:, None]
    place = lax.axis_index("space") * (2 * PAIRS) + first + own
    index = (named - place + 1) % 512 + own

    rightward, leftward = neighbour_moves(1), neighbour_moves(-1)
    pert_left = lax.ppermute(pert[:, 1], both, rightward)
    pert_right = lax.ppermute(pert[:, 0], both, leftward)
    field_left = lax.ppermute(field[:, 1], both, rightward)
    field_right = lax.ppermute(field[:, 0], both, leftward)

    members = NMEM * NMEM
    pair = jax.ShapeDtypeStruct((2, members, PV), BF16)
    turned = jax.ShapeDtypeStruct((2, PV, members), BF16)
    small = jax.ShapeDtypeStruct((2, PV, PV), F32)
    base = jax.ShapeDtypeStruct(packed, F32)
    half = pltpu.VMEM((2, members, PV), BF16)
    square = pltpu.VMEM((2, PV, PV), F32)
    scratch = [half, half] + [square] * 5
    scratch += [pltpu.VMEM((2, PV, 3 * PV), F32), pltpu.VMEM((2, members, PV), F32)]
    index = jnp.concatenate([index[:1, ::-1], index[1:]], axis=0)
    own_parts = vmem_call(
        own_kernel, [turned] * 4 + [pair] * 2 + [small] * 2 + [base], [half] * 4 + [square] * 2,
        smem=1, n_in=5, us=9,
    )(index, field, pert, slots, variances)
    analysis = vmem_call(update_kernel, packed, scratch, smem=1, n_in=18, us=7)(
        index, field, field_left, field_right, pert, pert_left, pert_right, slots, variances,
        *own_parts,
    )
    returned = lax.all_to_all(analysis, "mem", 0, 0, tiled=True)
    out = copying_call(
        from_sent_kernel, (rows, PV), pltpu.VMEM,
        [pltpu.VMEM((rows, PV), F32), pltpu.SemaphoreType.DMA((PIECES,))],
    )(returned.reshape(sent))
    return out.reshape(prior_sample_set.shape)


def solution(mesh):
    rows = P("space", None)
    cube = P("mem", "space", None)
    return jax.shard_map(
        body,
        mesh=mesh,
        in_specs=(cube, cube, rows, rows, rows, P(), P(), P(), P(), P()),
        out_specs=cube,
        check_vma=False,
    )
```

```python
import jax
import jax.numpy as jnp
from jax import lax
from jax.experimental import pallas as pl
from jax.experimental.pallas import tpu as pltpu
from jax.sharding import PartitionSpec as P

LEV = 64
HID = 512
HOPS = 2
PV = 128
NMEM = 32
PIECES = 4
WIDE = 100.0
PAIRS = 32
F32 = jnp.float32
BF16 = jnp.bfloat16


def owner_of(pair):
    chip, core = pair // 2, pair % 2
    z, x = (chip, 0) if chip < 8 else (15 - chip, 1)
    return (z * 2 + x) * 2 + core


def mirrored(run):
    return (run + 1 + run // 4) % 2


def pair_of(member, run):
    z, x, core = member // 4, (member // 2 + mirrored(run)) % 2, member % 2
    return 2 * jnp.where(x == 0, z, 15 - z) + core


def neighbour_moves(step):
    runs = 8

    def device(patches):
        run, pair = patches // PAIRS % runs, patches % PAIRS
        return (owner_of(pair) ^ 2 * mirrored(run)) * runs + run

    return [(device(here), device(here + step)) for here in range(runs * PAIRS)]


def dot(a, b):
    return jnp.dot(a, b, preferred_element_type=F32)


def dot_t(a, b):
    return lax.dot_general(a, b, (((1,), (1,)), ((), ())), preferred_element_type=F32)


def split(a):
    high = a.astype(BF16)
    return high, (a - high.astype(F32)).astype(BF16)


def dot3(a, b):
    (ah, al), (bh, bl) = split(a), split(b)
    return dot(ah, bh) + (dot(ah, bl) + dot(al, bh))


def row_shift():
    return 4 * mirrored(lax.axis_index("space"))


def sent_row(patch, shift):
    row = 2 * owner_of(patch // 2) + patch % 2
    return row - shift if row & 4 else row + shift


def to_send_kernel(x_ref, o_ref, came, put, in_sems, out_sems):
    shift = row_shift()
    group = 2 * PAIRS // PIECES
    for g in range(PIECES):
        part = pl.ds(g * group, group)
        pltpu.make_async_copy(x_ref.at[:, part], came.at[:, part], in_sems.at[g]).start()
    rows = came.reshape(2 * PAIRS * NMEM, PV)
    copies = []
    for g in range(PIECES):
        part = pl.ds(g * group, group)
        pltpu.make_async_copy(x_ref.at[:, part], came.at[:, part], in_sems.at[g]).wait()
        for chip in range(g * group // 4, (g + 1) * group // 4):
            for patch in range(4 * chip, 4 * chip + 4):
                put[sent_row(patch, shift)] = rows[pl.ds(patch, NMEM, stride=2 * PAIRS), :]
            part = pl.ds(sent_row(4 * chip, shift), 4)
            copies.append(pltpu.make_async_copy(put.at[part], o_ref.at[part], out_sems.at[chip]))
            copies[-1].start()
    for copy in copies:
        copy.wait()


def from_sent_kernel(x_ref, o_ref, put, sems):
    shift = row_shift()
    step = NMEM // PIECES
    copies = []
    for g in range(PIECES):
        first = g * step * 2 * PAIRS
        for patch in range(2 * PAIRS):
            put[pl.ds(first + patch, step, stride=2 * PAIRS), :] = x_ref[
                sent_row(patch, shift), g * step : (g + 1) * step
            ]
        part = pl.ds(first, step * 2 * PAIRS)
        copies.append(pltpu.make_async_copy(put.at[part], o_ref.at[part], sems.at[g]))
        copies[-1].start()
    for copy in copies:
        copy.wait()


def forecast_kernel(x_ref, g_ref, wi_ref, bi_ref, wo_ref, bo_ref, o_ref, wi2, wo2):
    for both, one in ((wi2, (wi_ref[...].astype(F32) * 0.5).astype(BF16)), (wo2, wo_ref[...])):
        zero = jnp.zeros_like(one)
        both[:LEV, :HID] = one
        both[:LEV, HID:] = zero
        both[LEV:, :HID] = zero
        both[LEV:, HID:] = one
    gain = jnp.concatenate([g_ref[...]] * 2, axis=1)
    bi = jnp.concatenate([bi_ref[...]] * 2, axis=1) * 0.5
    bo = jnp.concatenate([bo_ref[...]] * 2, axis=1)
    row = lax.broadcasted_iota(jnp.int32, (2 * PV, PV), 0)
    col = lax.broadcasted_iota(jnp.int32, (2 * PV, PV), 1)
    halves = jnp.where((row % PV) // LEV == col // LEV, 1.0, 0.0).astype(BF16)
    chunk, shift = PAIRS, row_shift()
    for first in range(0, 2 * PAIRS, chunk):
        x = jnp.concatenate(
            [x_ref[pl.ds(first + i, NMEM, stride=2 * PAIRS), :] for i in range(chunk)], axis=0
        )
        for _ in range(HOPS):
            squares = jnp.concatenate(split(x * x), axis=1)
            inverse = lax.rsqrt(dot(squares, halves) * (1.0 / LEV) + 1e-6)
            normed = (x * inverse * gain).astype(BF16)
            h = dot(normed, wi2[...]) + bi
            hidden = (h + h * jnp.tanh(h)).astype(BF16)
            x = x + dot_t(hidden, wo2[...]) + bo
        for i in range(chunk):
            patch = first + i
            o_ref[sent_row(patch, shift)] = x[i * NMEM : (i + 1) * NMEM]


def exact(a, b):
    return jnp.dot(a, b, precision=lax.Precision.HIGHEST, preferred_element_type=F32)


def observe(x, slots):
    slots = jnp.broadcast_to(slots, x.shape)
    return jnp.take_along_axis(x, slots, axis=1, mode="promise_in_bounds")


def centred(x):
    return x - jnp.mean(x, axis=0, keepdims=True)


def identity():
    row = lax.broadcasted_iota(jnp.int32, (PV, PV), 0)
    return jnp.where(row == lax.broadcasted_iota(jnp.int32, (PV, PV), 1), 1.0, 0.0)


def closer(delta):
    return delta * delta / (2.0 - delta * delta)


def sharper(s, x, delta, product=dot3):
    return (2.0 / (2.0 - delta * delta)) * (2.0 * x - product(x, product(s, x)))


def inverses(matrices, s_ref, x_ref, steps, goal):
    eye = identity()
    xs, deltas, tops = [], [], []
    for s in matrices:
        s2 = dot3(s, s)
        rows = jnp.max(jnp.sum(jnp.abs(s2), axis=0, keepdims=True), axis=1, keepdims=True)
        whole = jnp.sum(jnp.sum(s2 * s2, axis=0, keepdims=True), axis=1, keepdims=True)
        top = jnp.sqrt(jnp.minimum(rows, jnp.sqrt(whole)))
        c = 2.0 / (top + 1.0)
        delta = (top - 1.0) / (top + 1.0)
        mu = 2.0 / (2.0 - delta * delta)
        x1 = (mu * c) * (2.0 * eye - c * s)
        t1 = (mu * c) * (2.0 * s - c * s2)
        delta = closer(delta)
        xs.append((2.0 / (2.0 - delta * delta)) * (2.0 * x1 - dot3(x1, t1)))
        deltas.append(closer(delta))
        tops.append(jnp.max(top))
    for _ in range(steps):
        xs = [sharper(*it) for it in zip(matrices, xs, deltas)]
        deltas = [closer(delta) for delta in deltas]
    for j in range(2):
        s_ref[j] = matrices[j]
        x_ref[j] = xs[j]

    def more(state):
        return jnp.maximum(state[0], state[1]) > goal

    def sharpen(state):
        for j in range(2):
            x_ref[j] = sharper(s_ref[j], x_ref[j], state[j])
        return tuple(closer(delta) for delta in state)

    last = lax.while_loop(more, sharpen, tuple(jnp.max(delta) for delta in deltas))

    @pl.when(jnp.maximum(*tops) > WIDE)
    def _():
        for j in range(2):
            x_ref[j] = (2.0 / (tops[j] + 1.0)) * eye

            def once(delta, j=j):
                x_ref[j] = sharper(s_ref[j], x_ref[j], delta, exact)
                return closer(delta)

            start = (tops[j] - 1.0) / (tops[j] + 1.0)
            lax.while_loop(lambda delta: delta > 1e-4, once, once(start))
            x_ref[j] = 2.0 * x_ref[j] - exact(x_ref[j], exact(s_ref[j], x_ref[j]))

    return jnp.maximum(*last), jnp.maximum(*tops)


def own_kernel(
    idx_ref, f_ref, p_ref, slot_ref, var_ref,
    ath, atl, bth, btl, dh, dl, inv_ref, part_ref, base_ref, ah, al, bh, bl, s_ref, x_ref,
):
    members = NMEM * NMEM
    root = lax.rsqrt(var_ref[...])
    for w in range(2):
        x = f_ref[:, w].reshape(members, PV)
        y = observe(x, slot_ref[w + 1 : w + 2, :])
        r = root[w + 1 : w + 2, :]
        a, b = centred(x), centred(y) * r
        ah[w], al[w] = split(a)
        bh[w], bl[w] = split(b)
        ath[w], atl[w] = split(a.T)
        bth[w], btl[w] = split(b.T)
        dh[w], dl[w] = split((p_ref[:, w].reshape(members, PV) - y) * r)
    scale = 1.0 / (members - 1)
    matrices, crosses = [], []
    for j in range(2):
        o = idx_ref[j, 0] - 1
        high, low = bth[o], btl[o]
        mixed = dot(high, bl[o])
        small = mixed + (mixed.T + dot(low, bl[o]))
        matrices.append((dot(high, bh[o]) + small) * scale + identity())
        small = dot(high, al[j]) + (dot(low, ah[j]) + dot(low, al[j]))
        crosses.append((dot(high, ah[j]) + small) * scale)
    inverses(matrices, s_ref, x_ref, 3, 1e-4)
    for j in range(2):
        x = x_ref[j]
        inv_ref[j] = x
        part = exact(x, crosses[j])
        part_ref[j] = part
        o = idx_ref[j, 0] - 1
        ph, pl_ = split(part)
        gained = dot(dh[o], ph) + (dot(dh[o], pl_) + dot(dl[o], ph))
        base_ref[:, j] = f_ref[:, j] + gained.reshape(NMEM, NMEM, PV)


def update_kernel(
    idx_ref, f_ref, fl_ref, fr_ref, p_ref, pl_ref, pr_ref, slot_ref, var_ref,
    ath, atl, bth, btl, dh, dl, inv_ref, part_ref, base_ref, o_ref, hh, hl, s_ref, x_ref,
    g_ref, k_ref, link_ref, gram_ref, d_ref,
):
    members = NMEM * NMEM
    scale = 1.0 / (members - 1)
    fields, readings = (fl_ref, fr_ref), (pl_ref, pr_ref)
    norms = []
    for j in range(2):
        o, h = idx_ref[j, 0] - 1, idx_ref[j, 1]
        apart = h == 3 * j
        x = jnp.where(apart, fields[j][...], f_ref[:, j]).reshape(members, PV)
        p = jnp.where(apart, readings[j][...], p_ref[:, j]).reshape(members, PV)
        y = observe(x, slot_ref[pl.ds(h, 1), :])
        r = lax.rsqrt(var_ref[pl.ds(h, 1), :])
        b = centred(y) * r
        d_ref[j] = (p - y) * r
        rows = [bth[o], btl[o], *split(b.T), ath[j], atl[j]]
        both = dot(jnp.concatenate(rows, axis=0), jnp.concatenate(split(b), axis=1))
        both = both[:, :PV] + both[:, PV:]
        s_oh, s_hh, g = (both[n : n + PV] + both[n + PV : n + 2 * PV] for n in (0, 2 * PV, 4 * PV))
        gram = jnp.concatenate([s_oh.T, s_hh, g.T], axis=1) * scale
        gram_ref[j] = gram
        norms.append(jnp.sum(gram * gram))

    def eliminate(j, product):
        s_ho, s_hh, g_h = (gram_ref[j, :, n * PV : (n + 1) * PV] for n in range(3))
        link = product(s_ho, inv_ref[j])
        link_ref[j] = link
        s_ref[j] = s_hh + identity() - product(link, s_ho.T)
        g_ref[j] = g_h - product(s_ho, part_ref[j])

    for j in range(2):
        eliminate(j, dot3)

    @pl.when(jnp.maximum(*norms) > 300.0**2)
    def _():
        for j in range(2):
            eliminate(j, exact)

    for j in range(2):
        o = idx_ref[j, 0] - 1
        lh, ll = split(link_ref[j])
        carried = dot_t(dh[o], lh) + (dot_t(dh[o], ll) + dot_t(dl[o], lh))
        hh[j], hl[j] = split(d_ref[j] - carried)
    complements = [s_ref[j] for j in range(2)]
    delta, top = inverses(complements, s_ref, x_ref, 2, 0.01)
    for j in range(2):
        s, x, g = s_ref[j], x_ref[j], g_ref[j]
        k = dot3(x, g)
        k_ref[j] = k + dot3(x, g - dot3(s, k))

    @pl.when(jnp.maximum(delta * (WIDE / 0.0075), top) > WIDE)
    def _():
        for j in range(2):
            for _ in range(2):
                k_ref[j] += dot3(x_ref[j], g_ref[j] - exact(s_ref[j], k_ref[j]))

    for j in range(2):
        kh, kl = split(k_ref[j])
        gained = dot(hh[j], kh) + (dot(hh[j], kl) + dot(hl[j], kh))
        o_ref[:, j] = base_ref[:, j] + gained.reshape(NMEM, NMEM, PV)


def copying_call(kernel, out, space, scratch, limit=16):
    return pl.pallas_call(
        kernel,
        out_shape=jax.ShapeDtypeStruct(out, F32),
        in_specs=[pl.BlockSpec(memory_space=space)],
        out_specs=pl.BlockSpec(memory_space=pl.ANY),
        scratch_shapes=scratch,
        compiler_params=pltpu.CompilerParams(vmem_limit_bytes=limit << 20),
        cost_estimate=pl.CostEstimate(flops=10**9, bytes_accessed=2 << 20, transcendentals=0),
    )


def vmem_call(kernel, out, scratch=(), smem=0, limit=24, n_in=1, us=2):
    specs = [pl.BlockSpec(memory_space=pltpu.SMEM)] * smem
    specs += [pl.BlockSpec(memory_space=pltpu.VMEM)] * (n_in - smem)
    single = isinstance(out, tuple)
    shapes = jax.ShapeDtypeStruct(out, F32) if single else out
    return pl.pallas_call(
        kernel,
        out_shape=shapes,
        in_specs=specs,
        out_specs=jax.tree.map(lambda _: pl.BlockSpec(memory_space=pltpu.VMEM), shapes),
        scratch_shapes=list(scratch),
        compiler_params=pltpu.CompilerParams(vmem_limit_bytes=limit << 20),
        cost_estimate=pl.CostEstimate(
            flops=us * 10**9, bytes_accessed=1 << 20, transcendentals=0
        ),
    )


def body(
    prior_sample_set, perturbed_obs, measured_slot_table, obs_var, neighbours,
    norm_gain, w_in, b_in, w_out, b_out,
):
    rows = 2 * PAIRS * NMEM
    sent = (2 * PAIRS, NMEM, PV)
    packed = (NMEM, 2, NMEM, PV)
    both = ("mem", "space")
    first = 2 * pair_of(lax.axis_index("mem"), lax.axis_index("space"))

    pert_send = copying_call(
        to_send_kernel, sent, pl.ANY,
        [
            pltpu.VMEM(perturbed_obs.shape, F32), pltpu.VMEM(sent, F32),
            pltpu.SemaphoreType.DMA((PIECES,)), pltpu.SemaphoreType.DMA((PAIRS // 2,)),
        ],
        limit=60,
    )(perturbed_obs)
    pert = lax.all_to_all(pert_send.reshape(packed), "mem", 0, 0, tiled=True)

    field_send = vmem_call(
        forecast_kernel, sent,
        [pltpu.VMEM((2 * LEV, 2 * HID), BF16)] * 2, n_in=6, us=7,
    )(
        prior_sample_set.reshape(rows, PV), norm_gain.reshape(1, -1), w_in, b_in.reshape(1, -1),
        w_out.T, b_out.reshape(1, -1),
    )
    meta = jnp.concatenate([measured_slot_table.astype(F32), obs_var], axis=-1)
    field_send, meta = lax.optimization_barrier((field_send, meta))
    field = lax.all_to_all(field_send.reshape(packed), "mem", 0, 0, tiled=True)

    runs = [(i, (i + 1) % 8) for i in range(8)]
    before = lax.ppermute(meta[-1:], "space", runs)
    after = lax.ppermute(meta[:1], "space", [(j, i) for i, j in runs])
    window = lax.dynamic_slice_in_dim(
        jnp.concatenate([before, meta, after], axis=0), first, 4, 0
    )
    slots, variances = window[:, :PV].astype(jnp.int32), window[:, PV:]
    named = lax.dynamic_slice_in_dim(neighbours, first, 2, 0)
    own = jnp.arange(2, dtype=jnp.int32)[:, None]
    place = lax.axis_index("space") * (2 * PAIRS) + first + own
    index = (named - place + 1) % 512 + own

    rightward, leftward = neighbour_moves(1), neighbour_moves(-1)
    pert_left = lax.ppermute(pert[:, 1], both, rightward)
    pert_right = lax.ppermute(pert[:, 0], both, leftward)
    field_left = lax.ppermute(field[:, 1], both, rightward)
    field_right = lax.ppermute(field[:, 0], both, leftward)

    members = NMEM * NMEM
    pair = jax.ShapeDtypeStruct((2, members, PV), BF16)
    turned = jax.ShapeDtypeStruct((2, PV, members), BF16)
    small = jax.ShapeDtypeStruct((2, PV, PV), F32)
    base = jax.ShapeDtypeStruct(packed, F32)
    half = pltpu.VMEM((2, members, PV), BF16)
    square = pltpu.VMEM((2, PV, PV), F32)
    scratch = [half, half] + [square] * 5
    scratch += [pltpu.VMEM((2, PV, 3 * PV), F32), pltpu.VMEM((2, members, PV), F32)]
    index = jnp.concatenate([index[:1, ::-1], index[1:]], axis=0)
    own_parts = vmem_call(
        own_kernel, [turned] * 4 + [pair] * 2 + [small] * 2 + [base], [half] * 4 + [square] * 2,
        smem=1, n_in=5, us=9,
    )(index, field, pert, slots, variances)
    analysis = vmem_call(update_kernel, packed, scratch, smem=1, n_in=18, us=7)(
        index, field, field_left, field_right, pert, pert_left, pert_right, slots, variances,
        *own_parts,
    )
    returned = lax.all_to_all(analysis, "mem", 0, 0, tiled=True)
    out = copying_call(
        from_sent_kernel, (rows, PV), pltpu.VMEM,
        [pltpu.VMEM((rows, PV), F32), pltpu.SemaphoreType.DMA((PIECES,))],
    )(returned.reshape(sent))
    return out.reshape(prior_sample_set.shape)


def solution(mesh):
    rows = P("space", None)
    cube = P("mem", "space", None)
    return jax.shard_map(
        body,
        mesh=mesh,
        in_specs=(cube, cube, rows, rows, rows, P(), P(), P(), P(), P()),
        out_specs=cube,
        check_vma=False,
    )
```

```python
import jax
import jax.numpy as jnp
from jax import lax
from jax.experimental import pallas as pl
from jax.experimental.pallas import tpu as pltpu
from jax.sharding import PartitionSpec as P

LEV = 64
HID = 512
HOPS = 2
PV = 128
NMEM = 32
PIECES = 4
WIDE = 100.0
PAIRS = 32
F32 = jnp.float32
BF16 = jnp.bfloat16


def owner_of(pair):
    chip, core = pair // 2, pair % 2
    z, x = (chip, 0) if chip < 8 else (15 - chip, 1)
    return (z * 2 + x) * 2 + core


def mirrored(run):
    return (run + 1 + run // 4) % 2


def pair_of(member, run):
    z, x, core = member // 4, (member // 2 + mirrored(run)) % 2, member % 2
    return 2 * jnp.where(x == 0, z, 15 - z) + core


def neighbour_moves(step):
    runs = 8

    def device(patches):
        run, pair = patches // PAIRS % runs, patches % PAIRS
        return (owner_of(pair) ^ 2 * mirrored(run)) * runs + run

    return [(device(here), device(here + step)) for here in range(runs * PAIRS)]


def dot(a, b):
    return jnp.dot(a, b, preferred_element_type=F32)


def dot_t(a, b):
    return lax.dot_general(a, b, (((1,), (1,)), ((), ())), preferred_element_type=F32)


def split(a):
    high = a.astype(BF16)
    return high, (a - high.astype(F32)).astype(BF16)


def dot3(a, b):
    (ah, al), (bh, bl) = split(a), split(b)
    return dot(ah, bh) + (dot(ah, bl) + dot(al, bh))


def row_shift():
    return 4 * mirrored(lax.axis_index("space"))


def sent_row(patch, shift):
    row = 2 * owner_of(patch // 2) + patch % 2
    return row - shift if row & 4 else row + shift


def to_send_kernel(x_ref, o_ref, came, put, in_sems, out_sems):
    shift = row_shift()
    group = 2 * PAIRS // PIECES
    for g in range(PIECES):
        part = pl.ds(g * group, group)
        pltpu.make_async_copy(x_ref.at[:, part], came.at[:, part], in_sems.at[g]).start()
    rows = came.reshape(2 * PAIRS * NMEM, PV)
    copies = []
    for g in range(PIECES):
        part = pl.ds(g * group, group)
        pltpu.make_async_copy(x_ref.at[:, part], came.at[:, part], in_sems.at[g]).wait()
        for chip in range(g * group // 4, (g + 1) * group // 4):
            for patch in range(4 * chip, 4 * chip + 4):
                put[sent_row(patch, shift)] = rows[pl.ds(patch, NMEM, stride=2 * PAIRS), :]
            part = pl.ds(sent_row(4 * chip, shift), 4)
            copies.append(pltpu.make_async_copy(put.at[part], o_ref.at[part], out_sems.at[chip]))
            copies[-1].start()
    for copy in copies:
        copy.wait()


def from_sent_kernel(x_ref, o_ref, put, sems):
    shift = row_shift()
    step = NMEM // PIECES
    copies = []
    for g in range(PIECES):
        first = g * step * 2 * PAIRS
        for patch in range(2 * PAIRS):
            put[pl.ds(first + patch, step, stride=2 * PAIRS), :] = x_ref[
                sent_row(patch, shift), g * step : (g + 1) * step
            ]
        part = pl.ds(first, step * 2 * PAIRS)
        copies.append(pltpu.make_async_copy(put.at[part], o_ref.at[part], sems.at[g]))
        copies[-1].start()
    for copy in copies:
        copy.wait()


def forecast_kernel(x_ref, g_ref, wi_ref, bi_ref, wo_ref, bo_ref, o_ref, wi2, wo2):
    for both, one in ((wi2, (wi_ref[...].astype(F32) * 0.5).astype(BF16)), (wo2, wo_ref[...])):
        zero = jnp.zeros_like(one)
        both[:LEV, :HID] = one
        both[:LEV, HID:] = zero
        both[LEV:, :HID] = zero
        both[LEV:, HID:] = one
    gain = jnp.concatenate([g_ref[...]] * 2, axis=1)
    bi = jnp.concatenate([bi_ref[...]] * 2, axis=1) * 0.5
    bo = jnp.concatenate([bo_ref[...]] * 2, axis=1)
    row = lax.broadcasted_iota(jnp.int32, (2 * PV, PV), 0)
    col = lax.broadcasted_iota(jnp.int32, (2 * PV, PV), 1)
    halves = jnp.where((row % PV) // LEV == col // LEV, 1.0, 0.0).astype(BF16)
    chunk, shift = PAIRS, row_shift()
    for first in range(0, 2 * PAIRS, chunk):
        x = jnp.concatenate(
            [x_ref[pl.ds(first + i, NMEM, stride=2 * PAIRS), :] for i in range(chunk)], axis=0
        )
        for _ in range(HOPS):
            squares = jnp.concatenate(split(x * x), axis=1)
            inverse = lax.rsqrt(dot(squares, halves) * (1.0 / LEV) + 1e-6)
            normed = (x * inverse * gain).astype(BF16)
            h = dot(normed, wi2[...]) + bi
            hidden = (h + h * jnp.tanh(h)).astype(BF16)
            x = x + dot_t(hidden, wo2[...]) + bo
        for i in range(chunk):
            patch = first + i
            o_ref[sent_row(patch, shift)] = x[i * NMEM : (i + 1) * NMEM]


def exact(a, b):
    return jnp.dot(a, b, precision=lax.Precision.HIGHEST, preferred_element_type=F32)


def observe(x, slots):
    slots = jnp.broadcast_to(slots, x.shape)
    return jnp.take_along_axis(x, slots, axis=1, mode="promise_in_bounds")


def centred(x):
    return x - jnp.mean(x, axis=0, keepdims=True)


def identity():
    row = lax.broadcasted_iota(jnp.int32, (PV, PV), 0)
    return jnp.where(row == lax.broadcasted_iota(jnp.int32, (PV, PV), 1), 1.0, 0.0)


def closer(delta):
    return delta * delta / (2.0 - delta * delta)


def sharper(s, x, delta, product=dot3):
    return (2.0 / (2.0 - delta * delta)) * (2.0 * x - product(x, product(s, x)))


def inverses(matrices, s_ref, x_ref, steps, goal):
    eye = identity()
    xs, deltas, tops = [], [], []
    for s in matrices:
        s2 = dot3(s, s)
        rows = jnp.max(jnp.sum(jnp.abs(s2), axis=0, keepdims=True), axis=1, keepdims=True)
        whole = jnp.sum(jnp.sum(s2 * s2, axis=0, keepdims=True), axis=1, keepdims=True)
        top = jnp.sqrt(jnp.minimum(rows, jnp.sqrt(whole)))
        c = 2.0 / (top + 1.0)
        delta = (top - 1.0) / (top + 1.0)
        mu = 2.0 / (2.0 - delta * delta)
        x1 = (mu * c) * (2.0 * eye - c * s)
        t1 = (mu * c) * (2.0 * s - c * s2)
        delta = closer(delta)
        xs.append((2.0 / (2.0 - delta * delta)) * (2.0 * x1 - dot3(x1, t1)))
        deltas.append(closer(delta))
        tops.append(jnp.max(top))
    for _ in range(steps):
        xs = [sharper(*it) for it in zip(matrices, xs, deltas)]
        deltas = [closer(delta) for delta in deltas]
    for j in range(2):
        s_ref[j] = matrices[j]
        x_ref[j] = xs[j]

    def more(state):
        return jnp.maximum(state[0], state[1]) > goal

    def sharpen(state):
        for j in range(2):
            x_ref[j] = sharper(s_ref[j], x_ref[j], state[j])
        return tuple(closer(delta) for delta in state)

    lax.while_loop(more, sharpen, tuple(jnp.max(delta) for delta in deltas))

    @pl.when(jnp.maximum(*tops) > WIDE)
    def _():
        for j in range(2):
            x_ref[j] = (2.0 / (tops[j] + 1.0)) * eye

            def once(delta, j=j):
                x_ref[j] = sharper(s_ref[j], x_ref[j], delta, exact)
                return closer(delta)

            start = (tops[j] - 1.0) / (tops[j] + 1.0)
            lax.while_loop(lambda delta: delta > 1e-4, once, once(start))
            x_ref[j] = 2.0 * x_ref[j] - exact(x_ref[j], exact(s_ref[j], x_ref[j]))

    return jnp.maximum(*tops)


def own_kernel(
    idx_ref, f_ref, p_ref, slot_ref, var_ref,
    ath, atl, bth, btl, dh, dl, inv_ref, part_ref, base_ref, ah, al, bh, bl, s_ref, x_ref,
):
    members = NMEM * NMEM
    root = lax.rsqrt(var_ref[...])
    for w in range(2):
        x = f_ref[:, w].reshape(members, PV)
        y = observe(x, slot_ref[w + 1 : w + 2, :])
        r = root[w + 1 : w + 2, :]
        a, b = centred(x), centred(y) * r
        ah[w], al[w] = split(a)
        bh[w], bl[w] = split(b)
        ath[w], atl[w] = split(a.T)
        bth[w], btl[w] = split(b.T)
        dh[w], dl[w] = split((p_ref[:, w].reshape(members, PV) - y) * r)
    scale = 1.0 / (members - 1)
    matrices, crosses = [], []
    for j in range(2):
        o = idx_ref[j, 0] - 1
        high, low = bth[o], btl[o]
        mixed = dot(high, bl[o])
        small = mixed + (mixed.T + dot(low, bl[o]))
        matrices.append((dot(high, bh[o]) + small) * scale + identity())
        small = dot(high, al[j]) + (dot(low, ah[j]) + dot(low, al[j]))
        crosses.append((dot(high, ah[j]) + small) * scale)
    inverses(matrices, s_ref, x_ref, 3, 1e-4)
    for j in range(2):
        x = x_ref[j]
        inv_ref[j] = x
        part = exact(x, crosses[j])
        part_ref[j] = part
        o = idx_ref[j, 0] - 1
        ph, pl_ = split(part)
        gained = dot(dh[o], ph) + (dot(dh[o], pl_) + dot(dl[o], ph))
        base_ref[:, j] = f_ref[:, j] + gained.reshape(NMEM, NMEM, PV)


def update_kernel(
    idx_ref, f_ref, fl_ref, fr_ref, p_ref, pl_ref, pr_ref, slot_ref, var_ref,
    ath, atl, bth, btl, dh, dl, inv_ref, part_ref, base_ref, o_ref, hh, hl, s_ref, x_ref,
    g_ref, k_ref, link_ref, gram_ref, d_ref,
):
    members = NMEM * NMEM
    scale = 1.0 / (members - 1)
    fields, readings = (fl_ref, fr_ref), (pl_ref, pr_ref)
    norms = []
    for j in range(2):
        o, h = idx_ref[j, 0] - 1, idx_ref[j, 1]
        apart = h == 3 * j
        x = jnp.where(apart, fields[j][...], f_ref[:, j]).reshape(members, PV)
        p = jnp.where(apart, readings[j][...], p_ref[:, j]).reshape(members, PV)
        y = observe(x, slot_ref[pl.ds(h, 1), :])
        r = lax.rsqrt(var_ref[pl.ds(h, 1), :])
        b = centred(y) * r
        d_ref[j] = (p - y) * r
        rows = [bth[o], btl[o], *split(b.T), ath[j], atl[j]]
        both = dot(jnp.concatenate(rows, axis=0), jnp.concatenate(split(b), axis=1))
        both = both[:, :PV] + both[:, PV:]
        s_oh, s_hh, g = (both[n : n + PV] + both[n + PV : n + 2 * PV] for n in (0, 2 * PV, 4 * PV))
        gram = jnp.concatenate([s_oh.T, s_hh, g.T], axis=1) * scale
        gram_ref[j] = gram
        norms.append(jnp.sum(gram * gram))

    def eliminate(j, product):
        s_ho, s_hh, g_h = (gram_ref[j, :, n * PV : (n + 1) * PV] for n in range(3))
        link = product(s_ho, inv_ref[j])
        link_ref[j] = link
        s_ref[j] = s_hh + identity() - product(link, s_ho.T)
        g_ref[j] = g_h - product(s_ho, part_ref[j])

    for j in range(2):
        eliminate(j, dot3)

    @pl.when(jnp.maximum(*norms) > 300.0**2)
    def _():
        for j in range(2):
            eliminate(j, exact)

    for j in range(2):
        o = idx_ref[j, 0] - 1
        lh, ll = split(link_ref[j])
        carried = dot_t(dh[o], lh) + (dot_t(dh[o], ll) + dot_t(dl[o], lh))
        hh[j], hl[j] = split(d_ref[j] - carried)
    complements = [s_ref[j] for j in range(2)]
    top = inverses(complements, s_ref, x_ref, 3, 1e-4)
    for j in range(2):
        k_ref[j] = dot3(x_ref[j], g_ref[j])

    @pl.when(top > WIDE)
    def _():
        for j in range(2):
            for _ in range(2):
                k_ref[j] += dot3(x_ref[j], g_ref[j] - exact(s_ref[j], k_ref[j]))

    for j in range(2):
        kh, kl = split(k_ref[j])
        gained = dot(hh[j], kh) + (dot(hh[j], kl) + dot(hl[j], kh))
        o_ref[:, j] = base_ref[:, j] + gained.reshape(NMEM, NMEM, PV)


def copying_call(kernel, out, space, scratch, limit=16):
    return pl.pallas_call(
        kernel,
        out_shape=jax.ShapeDtypeStruct(out, F32),
        in_specs=[pl.BlockSpec(memory_space=space)],
        out_specs=pl.BlockSpec(memory_space=pl.ANY),
        scratch_shapes=scratch,
        compiler_params=pltpu.CompilerParams(vmem_limit_bytes=limit << 20),
        cost_estimate=pl.CostEstimate(flops=10**9, bytes_accessed=2 << 20, transcendentals=0),
    )


def vmem_call(kernel, out, scratch=(), smem=0, limit=24, n_in=1, us=2):
    specs = [pl.BlockSpec(memory_space=pltpu.SMEM)] * smem
    specs += [pl.BlockSpec(memory_space=pltpu.VMEM)] * (n_in - smem)
    single = isinstance(out, tuple)
    shapes = jax.ShapeDtypeStruct(out, F32) if single else out
    return pl.pallas_call(
        kernel,
        out_shape=shapes,
        in_specs=specs,
        out_specs=jax.tree.map(lambda _: pl.BlockSpec(memory_space=pltpu.VMEM), shapes),
        scratch_shapes=list(scratch),
        compiler_params=pltpu.CompilerParams(vmem_limit_bytes=limit << 20),
        cost_estimate=pl.CostEstimate(
            flops=us * 10**9, bytes_accessed=1 << 20, transcendentals=0
        ),
    )


def body(
    prior_sample_set, perturbed_obs, measured_slot_table, obs_var, neighbours,
    norm_gain, w_in, b_in, w_out, b_out,
):
    rows = 2 * PAIRS * NMEM
    sent = (2 * PAIRS, NMEM, PV)
    packed = (NMEM, 2, NMEM, PV)
    both = ("mem", "space")
    first = 2 * pair_of(lax.axis_index("mem"), lax.axis_index("space"))

    pert_send = copying_call(
        to_send_kernel, sent, pl.ANY,
        [
            pltpu.VMEM(perturbed_obs.shape, F32), pltpu.VMEM(sent, F32),
            pltpu.SemaphoreType.DMA((PIECES,)), pltpu.SemaphoreType.DMA((PAIRS // 2,)),
        ],
        limit=60,
    )(perturbed_obs)
    pert = lax.all_to_all(pert_send.reshape(packed), "mem", 0, 0, tiled=True)

    field_send = vmem_call(
        forecast_kernel, sent,
        [pltpu.VMEM((2 * LEV, 2 * HID), BF16)] * 2, n_in=6, us=7,
    )(
        prior_sample_set.reshape(rows, PV), norm_gain.reshape(1, -1), w_in, b_in.reshape(1, -1),
        w_out.T, b_out.reshape(1, -1),
    )
    meta = jnp.concatenate([measured_slot_table.astype(F32), obs_var], axis=-1)
    field_send, meta = lax.optimization_barrier((field_send, meta))
    field = lax.all_to_all(field_send.reshape(packed), "mem", 0, 0, tiled=True)

    runs = [(i, (i + 1) % 8) for i in range(8)]
    before = lax.ppermute(meta[-1:], "space", runs)
    after = lax.ppermute(meta[:1], "space", [(j, i) for i, j in runs])
    window = lax.dynamic_slice_in_dim(
        jnp.concatenate([before, meta, after], axis=0), first, 4, 0
    )
    slots, variances = window[:, :PV].astype(jnp.int32), window[:, PV:]
    named = lax.dynamic_slice_in_dim(neighbours, first, 2, 0)
    own = jnp.arange(2, dtype=jnp.int32)[:, None]
    place = lax.axis_index("space") * (2 * PAIRS) + first + own
    index = (named - place + 1) % 512 + own

    rightward, leftward = neighbour_moves(1), neighbour_moves(-1)
    pert_left = lax.ppermute(pert[:, 1], both, rightward)
    pert_right = lax.ppermute(pert[:, 0], both, leftward)
    field_left = lax.ppermute(field[:, 1], both, rightward)
    field_right = lax.ppermute(field[:, 0], both, leftward)

    members = NMEM * NMEM
    pair = jax.ShapeDtypeStruct((2, members, PV), BF16)
    turned = jax.ShapeDtypeStruct((2, PV, members), BF16)
    small = jax.ShapeDtypeStruct((2, PV, PV), F32)
    base = jax.ShapeDtypeStruct(packed, F32)
    half = pltpu.VMEM((2, members, PV), BF16)
    square = pltpu.VMEM((2, PV, PV), F32)
    scratch = [half, half] + [square] * 5
    scratch += [pltpu.VMEM((2, PV, 3 * PV), F32), pltpu.VMEM((2, members, PV), F32)]
    index = jnp.concatenate([index[:1, ::-1], index[1:]], axis=0)
    own_parts = vmem_call(
        own_kernel, [turned] * 4 + [pair] * 2 + [small] * 2 + [base], [half] * 4 + [square] * 2,
        smem=1, n_in=5, us=9,
    )(index, field, pert, slots, variances)
    analysis = vmem_call(update_kernel, packed, scratch, smem=1, n_in=18, us=7)(
        index, field, field_left, field_right, pert, pert_left, pert_right, slots, variances,
        *own_parts,
    )
    returned = lax.all_to_all(analysis, "mem", 0, 0, tiled=True)
    out = copying_call(
        from_sent_kernel, (rows, PV), pltpu.VMEM,
        [pltpu.VMEM((rows, PV), F32), pltpu.SemaphoreType.DMA((PIECES,))],
    )(returned.reshape(sent))
    return out.reshape(prior_sample_set.shape)


def solution(mesh):
    rows = P("space", None)
    cube = P("mem", "space", None)
    return jax.shard_map(
        body,
        mesh=mesh,
        in_specs=(cube, cube, rows, rows, rows, P(), P(), P(), P(), P()),
        out_specs=cube,
        check_vma=False,
    )
```
